32 devices in a mesh: parts: 2 (over y), seq: 4 (over z), chan: 2 (over x), sub: 2 (over core).
Axes of the slice: x: 2, y: 2, z: 4, core: 2. Of those that a mesh axis runs over, the one named last changes fastest.
Arguments:
- signal: float32 [16, 16384], P(('parts', 'chan', 'sub'), 'seq'), parts along dimension 0, may hold values from -1 to 1
- filter_taps: float32 [16, 16384], P(('parts', 'chan', 'sub'), 'seq'), parts along dimension 0, may hold values from -4 to 4
- grad_out: float32 [16, 16384], P(('parts', 'chan', 'sub'), 'seq'), parts along dimension 0, may hold values from -6 to 6
- skip: float32 [16], P(('parts', 'chan', 'sub')), parts along dimension 0, may hold values from -4 to 4
Outputs:
- grad_signal: float32 [16, 16384], P(('parts', 'chan', 'sub'), 'seq'), parts along dimension 0
- grad_filter: float32 [16, 16384], P(('parts', 'chan', 'sub'), 'seq'), parts along dimension 0
- grad_skip: float32 [16], P(('parts', 'chan', 'sub')), parts along dimension 0
The draws below stay inside these ranges and needn't reach their ends.
There are 2 independent parts, one for each index of `parts`. The reference program is written for one: setup_inputs(seed, part) draws one part's arguments, and reference() takes and returns one part's arrays. A program takes and returns all parts, laid end to end along the dimension named above; each array names one. Nothing has to cross between parts.
All inputs are finite; a program needn't handle non-finite values.
Results may differ from the reference program's by a relative error of at most 0.00013.
Values sent between devices are 32-bit elements; how exact they have to be, the bound alone decides.
No kernel may reach another device: no remote copies, remote signals or barrier semaphores. Data moves between devices by JAX's collectives and lax.ppermute only.
A program may use at most 64 MiB of HBM per device.

```python
import math
import jax
import jax.numpy as jnp

CHANNELS = 8
SEQ = 16384


def draw_signal(key, part):
    key_base = jax.random.fold_in(jax.random.fold_in(key, 11), 0)
    position = jnp.arange(SEQ, dtype=jnp.float32)
    envelope = 1.0 + 2.0 * position / SEQ
    base = jnp.clip(jax.random.normal(key_base, (CHANNELS, SEQ), jnp.float32), -4.0, 4.0)
    return (base * envelope[None, :] / math.sqrt(SEQ)).astype(jnp.float32)


def draw_filter_taps(key, part):
    key_taps, key_pick, key_slow, key_fast = jax.random.split(jax.random.fold_in(key, 23), 4)
    position = jnp.arange(SEQ, dtype=jnp.float32)
    pick = jax.random.uniform(key_pick, (CHANNELS, 1), jnp.float32)
    slow_rate = jax.random.uniform(key_slow, (CHANNELS, 1), jnp.float32, 0.3, 2.0) / SEQ
    fast_rate = jnp.exp(jax.random.uniform(key_fast, (CHANNELS, 1), jnp.float32, math.log(2.0 / SEQ), math.log(1.0 / 30.0)))
    rate = jnp.where(pick < 0.5, slow_rate, fast_rate)
    taps = jnp.clip(jax.random.normal(key_taps, (CHANNELS, SEQ), jnp.float32), -4.0, 4.0)
    energy = jnp.expm1(-2.0 * rate * SEQ) / jnp.expm1(-2.0 * rate)
    return (taps * jnp.exp(-rate * position[None, :]) / jnp.sqrt(energy)).astype(jnp.float32)


def steps_of(own_key, shape, cuts, low, high):
    factor_of = 1.0
    for dim, shards_of in cuts:
        steps = jax.random.uniform(jax.random.fold_in(jax.random.fold_in(own_key, 6), dim), (shards_of,), jnp.float32, low / len(cuts), high / len(cuts))
        factor_of = factor_of * jnp.repeat(jnp.exp(steps), shape[dim] // shards_of).reshape((-1,) + (1,) * (len(shape) - 1 - dim))
    return factor_of


def gaussian(rng, extent, width, most, pieces=(), held_as=jnp.bfloat16):
    drawn = width * jax.random.normal(rng, extent, jnp.float32)
    if pieces:
        drawn = drawn * steps_of(rng, extent, pieces, -0.22, 0.18)
    return jnp.clip(drawn, -most, most).astype(held_as)


def setup_inputs(seed: int = 0, part: int = 0) -> dict:
    key_list = jax.random.split(jax.random.key(seed), 5)
    part_keys = jax.random.split(jax.random.fold_in(key_list[4], part), 5)
    return {
        "signal": draw_signal(jax.random.fold_in(jax.random.fold_in(key_list[4], part), 71), part),
        "filter_taps": draw_filter_taps(jax.random.fold_in(jax.random.fold_in(key_list[4], part), 71), part),
        "grad_out": gaussian(part_keys[2], (CHANNELS, SEQ), 1.0, 6.0, ((0, 4), (1, 4)), jnp.float32),
        "skip": gaussian(part_keys[3], (CHANNELS,), 1.0, 4.0, ((0, 4),), jnp.float32),
    }


def reference(signal, filter_taps, grad_out, skip):
    length = 2 * SEQ
    spec_signal = jnp.fft.rfft(signal, n=length, axis=1)
    spec_filter = jnp.fft.rfft(filter_taps, n=length, axis=1)
    spec_grad = jnp.fft.rfft(grad_out, n=length, axis=1)
    corr_input = jnp.fft.irfft(jnp.conj(spec_filter) * spec_grad, n=length, axis=1)[:, :SEQ]
    corr_filter = jnp.fft.irfft(jnp.conj(spec_signal) * spec_grad, n=length, axis=1)[:, :SEQ]
    grad_signal = corr_input.astype(signal.dtype) + skip[:, None] * grad_out
    grad_filter = corr_filter.astype(signal.dtype)
    grad_skip = jnp.sum(grad_out * signal, axis=1)
    return grad_signal, grad_filter, grad_skip
```

```python
import functools
import math

import jax
import jax.numpy as jnp
import ml_dtypes
import numpy as np
from jax import lax
from jax.experimental import pallas as pl
from jax.experimental.pallas import tpu as pltpu
from jax.sharding import PartitionSpec as P

LANES = 128
highest = lax.Precision.HIGHEST


def split_table(table):
    high = table.astype(np.float32).astype(ml_dtypes.bfloat16)
    low = (table - high.astype(np.float64)).astype(np.float32).astype(ml_dtypes.bfloat16)
    return high, low


def gathered_tables(length, channels, groups):
    rows = length // LANES
    coarse = np.arange(rows, dtype=np.float64)
    fine = np.arange(LANES, dtype=np.float64)
    phase = 2.0 * np.pi / rows * (coarse[:, None] + 0.25) * coarse[None, :]
    eye = np.eye(channels)
    forward = np.stack([np.cos(phase), -np.sin(phase)])
    first = np.einsum("cd,rjn->crjnd", eye, forward).reshape(channels * 2 * rows, rows * channels)
    last = first.T.reshape(groups, rows // groups * channels, channels * 2 * rows) / length
    turn = 2.0 * np.pi / length * (coarse[:, None] + 0.25) * fine[None, :]
    twiddle = np.stack([np.cos(turn), np.sin(turn)]).astype(np.float32)
    angle = 2.0 * np.pi / LANES * fine[:, None] * fine[None, :]
    cos, sin = np.cos(angle), np.sin(angle)
    second = np.block([[cos, -sin], [sin, cos]])
    third = np.block([[cos, sin], [-sin, cos]])
    return (*split_table(first), twiddle, *split_table(second), *split_table(third), *split_table(last))


def split(value):
    high = value.astype(jnp.bfloat16)
    return high, (value - high.astype(jnp.float32)).astype(jnp.bfloat16)


def product(left, right):
    dot = functools.partial(jnp.dot, preferred_element_type=jnp.float32)
    return dot(left[0], right[0]) + dot(left[0], right[1]) + dot(left[1], right[0])


def gathered_kernel(groups, channels, rows, skip_ref, *refs):
    blocks = refs[:groups]
    first_high, first_low, twiddle, second_high, second_low, third_high, third_low, last_high, last_low = refs[
        groups : groups + 9
    ]
    grad_signal_ref, grad_filter_ref, grad_skip_ref = refs[groups + 9 : groups + 12]
    data_high, data_low = refs[groups + 12 :]
    device = lax.axis_index("seq")
    height = rows // groups * channels
    total = jnp.zeros((height, LANES), jnp.float32)
    for step, block in enumerate(blocks):
        start = pl.multiple_of(lax.bitwise_xor(device, step) * height, height)
        value = block[...]
        total += value[:, LANES : 2 * LANES] * value[:, 2 * LANES :]
        high, low = split(value)
        data_high[pl.ds(start, height)] = high
        data_low[pl.ds(start, height)] = low
    owner = lax.broadcasted_iota(jnp.int32, (height, LANES), 0) % channels
    skip_rows = jnp.zeros((height, LANES), jnp.float32)
    for channel in range(channels):
        grad_skip_ref[channel] = jnp.sum(jnp.where(owner == channel, total, 0.0))
        skip_rows = jnp.where(owner == channel, skip_ref[channel], skip_rows)

    coarse = product((first_high[...], first_low[...]), (data_high[...], data_low[...]))
    cos, sin = twiddle[0], twiddle[1]
    turned = []
    for channel in range(channels):
        for array in range(3):
            lanes = slice(array * LANES, (array + 1) * LANES)
            real = coarse[2 * channel * rows : (2 * channel + 1) * rows, lanes]
            imag = coarse[(2 * channel + 1) * rows : (2 * channel + 2) * rows, lanes]
            turned.append(jnp.concatenate([real * cos + imag * sin, imag * cos - real * sin], axis=1))
    spectra = product(split(jnp.concatenate(turned)), (second_high[...], second_low[...]))
    products = []
    for channel in range(channels):
        grad = spectra[(3 * channel + 2) * rows : (3 * channel + 3) * rows]
        grad_real, grad_imag = grad[:, :LANES], grad[:, LANES:]
        for array in range(2):
            other = spectra[(3 * channel + array) * rows : (3 * channel + array + 1) * rows]
            real, imag = other[:, :LANES], other[:, LANES:]
            products.append(
                jnp.concatenate([real * grad_real + imag * grad_imag, real * grad_imag - imag * grad_real], axis=1)
            )
    back = product(split(jnp.concatenate(products)), (third_high[...], third_low[...]))
    columns = []
    for array in range(2):
        pieces = []
        for channel in range(channels):
            value = back[(2 * channel + array) * rows : (2 * channel + array + 1) * rows]
            real, imag = value[:, :LANES], value[:, LANES:]
            pieces += [real * cos - imag * sin, imag * cos + real * sin]
        columns.append(jnp.concatenate(pieces))
    result = product((last_high[0], last_low[0]), split(jnp.concatenate(columns, axis=1)))
    grad_signal_ref[...] = result[:, :LANES] + skip_rows * blocks[0][:, 2 * LANES :]
    grad_filter_ref[...] = result[:, LANES:]


def dense(value):
    channels, cells = value.shape
    return value.reshape(channels, cells // LANES, LANES).transpose(1, 0, 2).reshape(-1, LANES)


def undense(value, channels):
    return value.reshape(-1, channels, LANES).transpose(1, 0, 2).reshape(channels, -1)


def gathered_body(signal, filter_taps, grad_out, skip):
    groups = lax.axis_size("seq")
    channels, cells = signal.shape
    length = cells * groups
    rows = length // LANES
    height = rows // groups * channels
    own = jnp.concatenate([dense(filter_taps), dense(signal), dense(grad_out)], axis=1)
    blocks = [own]
    for step in range(1, groups):
        blocks.append(lax.ppermute(own, "seq", [(index, index ^ step) for index in range(groups)]))
    tables = gathered_tables(length, channels, groups)
    device = lax.axis_index("seq")
    whole = pl.BlockSpec(memory_space=pltpu.VMEM)
    last = [lax.dynamic_slice_in_dim(jnp.asarray(table), device, 1) for table in tables[-2:]]
    grad_signal, grad_filter, grad_skip = pl.pallas_call(
        functools.partial(gathered_kernel, groups, channels, rows),
        out_shape=(
            jax.ShapeDtypeStruct((height, LANES), jnp.float32),
            jax.ShapeDtypeStruct((height, LANES), jnp.float32),
            jax.ShapeDtypeStruct((channels,), jnp.float32),
        ),
        in_specs=[pl.BlockSpec(memory_space=pltpu.SMEM)] + [whole] * (groups + 9),
        out_specs=(whole, whole, pl.BlockSpec(memory_space=pltpu.SMEM)),
        scratch_shapes=[
            pltpu.VMEM((rows * channels, 3 * LANES), jnp.bfloat16),
            pltpu.VMEM((rows * channels, 3 * LANES), jnp.bfloat16),
        ],
        compiler_params=pltpu.CompilerParams(vmem_limit_bytes=24 * 2**20),
        name="correlate",
    )(skip, *blocks, *[jnp.asarray(table) for table in tables[:-2]], *last)
    return (undense(grad_signal, channels), undense(grad_filter, channels), grad_skip)


def frequency_order(groups):
    slots = jnp.arange(2 * groups, dtype=jnp.int32)
    halves = slots // 2
    return jnp.where(slots % 2 == 0, halves, jnp.where(halves == 0, groups, 2 * groups - halves))


def phase_table(left_index, right_index, period):
    product = left_index[:, None] * right_index[None, :] % period
    return 2.0 * math.pi / period * product.astype(jnp.float32)


def transform_tables(cells):
    inner_len = 128
    outer_len = cells // inner_len
    outer_range = jnp.arange(outer_len, dtype=jnp.int32)
    inner_range = jnp.arange(inner_len, dtype=jnp.int32)
    outer_phase = phase_table(outer_range, outer_range, outer_len)
    twist_phase = phase_table(outer_range, inner_range, cells)
    inner_phase = phase_table(inner_range, inner_range, inner_len)
    return (
        jnp.cos(outer_phase),
        jnp.sin(outer_phase),
        jnp.cos(twist_phase),
        jnp.sin(twist_phase),
        jnp.cos(inner_phase),
        jnp.sin(inner_phase),
    )


def complex_apply(real_part, imag_part, cos_table, sin_table, pattern, turning):
    first = jnp.einsum(pattern, real_part, cos_table, precision=highest) - turning * jnp.einsum(
        pattern, imag_part, sin_table, precision=highest
    )
    second = jnp.einsum(pattern, imag_part, cos_table, precision=highest) + turning * jnp.einsum(
        pattern, real_part, sin_table, precision=highest
    )
    return (first, second)


def forward_transform(real_part, imag_part, tables):
    outer_cos, outer_sin, twist_cos, twist_sin, inner_cos, inner_sin = tables
    outer_len = outer_cos.shape[0]
    inner_len = inner_cos.shape[0]
    initial = real_part.shape
    folded = initial[:-1] + (outer_len, inner_len)
    real_part = real_part.reshape(folded)
    imag_part = imag_part.reshape(folded)
    real_part, imag_part = complex_apply(
        real_part, imag_part, outer_cos, outer_sin, "...ab,ac->...cb", -1.0
    )
    real_part, imag_part = (
        real_part * twist_cos + imag_part * twist_sin,
        imag_part * twist_cos - real_part * twist_sin,
    )
    real_part, imag_part = complex_apply(
        real_part, imag_part, inner_cos, inner_sin, "...cb,bd->...cd", -1.0
    )
    return (real_part.reshape(initial), imag_part.reshape(initial))


def inverse_transform(real_part, imag_part, tables):
    outer_cos, outer_sin, twist_cos, twist_sin, inner_cos, inner_sin = tables
    outer_len = outer_cos.shape[0]
    inner_len = inner_cos.shape[0]
    initial = real_part.shape
    folded = initial[:-1] + (outer_len, inner_len)
    real_part = real_part.reshape(folded)
    imag_part = imag_part.reshape(folded)
    real_part, imag_part = complex_apply(
        real_part, imag_part, inner_cos, inner_sin, "...cd,bd->...cb", 1.0
    )
    real_part, imag_part = (
        real_part * twist_cos - imag_part * twist_sin,
        imag_part * twist_cos + real_part * twist_sin,
    )
    real_part, imag_part = complex_apply(
        real_part, imag_part, outer_cos, outer_sin, "...cb,ac->...ab", 1.0
    )
    return (real_part.reshape(initial), imag_part.reshape(initial))


def split_body(signal, filter_taps, grad_out, skip):
    groups = lax.axis_size("seq")
    device = lax.axis_index("seq")
    cells = signal.shape[1]
    width = cells // groups
    doubled = 2 * groups
    period = doubled * cells
    freq_slots = frequency_order(groups)
    tables = transform_tables(cells)
    stacked = jnp.stack([signal, filter_taps, grad_out])[:, :, None, :]
    columns = lax.all_to_all(stacked, "seq", split_axis=3, concat_axis=2, tiled=True)
    group_rows = jnp.arange(groups, dtype=jnp.int32)
    group_phase = phase_table(group_rows, freq_slots, doubled)
    group_cos = jnp.cos(group_phase)
    group_sin = jnp.sin(group_phase)
    real_part = jnp.einsum("acpj,pm->acmj", columns, group_cos, precision=highest)
    imag_part = -jnp.einsum("acpj,pm->acmj", columns, group_sin, precision=highest)
    residues = device * width + jnp.arange(width, dtype=jnp.int32)
    twist_phase = phase_table(freq_slots, residues, period)
    twist_cos = jnp.cos(twist_phase)
    twist_sin = jnp.sin(twist_phase)
    twisted_real = real_part * twist_cos + imag_part * twist_sin
    twisted_imag = imag_part * twist_cos - real_part * twist_sin
    outgoing = jnp.stack([twisted_real, twisted_imag], 1)
    spectra = lax.all_to_all(outgoing, "seq", split_axis=3, concat_axis=4, tiled=True)
    freq_real, freq_imag = forward_transform(spectra[:, 0], spectra[:, 1], tables)
    grad_real = freq_real[-1]
    grad_imag = freq_imag[-1]
    signal_real, signal_imag = (freq_real[0], freq_imag[0])
    filter_real, filter_imag = (freq_real[1], freq_imag[1])
    input_real = filter_real * grad_real + filter_imag * grad_imag
    input_imag = filter_real * grad_imag - filter_imag * grad_real
    taps_real = signal_real * grad_real + signal_imag * grad_imag
    taps_imag = signal_real * grad_imag - signal_imag * grad_real
    back_real = jnp.stack([input_real, taps_real])
    back_imag = jnp.stack([input_imag, taps_imag])
    inverse_real, inverse_imag = inverse_transform(back_real, back_imag, tables)
    full_range = jnp.arange(cells, dtype=jnp.int32)
    local_slots = lax.dynamic_slice_in_dim(freq_slots, 2 * device, 2)
    back_phase = phase_table(local_slots, full_range, period)
    back_cos = jnp.cos(back_phase)
    back_sin = jnp.sin(back_phase)
    turned_real = inverse_real * back_cos - inverse_imag * back_sin
    turned_imag = inverse_imag * back_cos + inverse_real * back_sin
    returning = jnp.stack([turned_real, turned_imag], 1)
    residue_rows = lax.all_to_all(returning, "seq", split_axis=4, concat_axis=3, tiled=True)
    scale = 1.0 / period
    real_out = (
        jnp.einsum("ncmj,pm->ncpj", residue_rows[:, 0], group_cos, precision=highest)
        - jnp.einsum("ncmj,pm->ncpj", residue_rows[:, 1], group_sin, precision=highest)
    ) * scale
    gathered = lax.all_to_all(real_out, "seq", split_axis=2, concat_axis=3, tiled=True)
    grad_signal = gathered[0, :, 0, :] + skip[:, None] * grad_out
    grad_filter = gathered[1, :, 0, :]
    grad_skip = lax.psum(jnp.sum(grad_out * signal, axis=1), "seq")
    return (grad_signal, grad_filter, grad_skip)


def body(signal, filter_taps, grad_out, skip):
    groups = lax.axis_size("seq")
    channels, cells = signal.shape
    whole_fits = channels * cells * groups <= 2**15
    if whole_fits and groups & (groups - 1) == 0 and cells % (16 * LANES) == 0:
        return gathered_body(signal, filter_taps, grad_out, skip)
    return split_body(signal, filter_taps, grad_out, skip)
def solution(mesh):
    return jax.shard_map(
        body,
        mesh=mesh,
        in_specs=(
            P(("parts", "chan", "sub"), "seq"),
            P(("parts", "chan", "sub"), "seq"),
            P(("parts", "chan", "sub"), "seq"),
            P(("parts", "chan", "sub")),
        ),
        out_specs=(
            P(("parts", "chan", "sub"), "seq"),
            P(("parts", "chan", "sub"), "seq"),
            P(("parts", "chan", "sub")),
        ),
        check_vma=False,
    )
```

```python
import functools
import math

import jax
import jax.numpy as jnp
import ml_dtypes
import numpy as np
from jax import lax
from jax.experimental import pallas as pl
from jax.experimental.pallas import tpu as pltpu
from jax.sharding import PartitionSpec as P

LANES = 128
highest = lax.Precision.HIGHEST


def split_table(table):
    high = table.astype(np.float32).astype(ml_dtypes.bfloat16)
    low = (table - high.astype(np.float64)).astype(np.float32).astype(ml_dtypes.bfloat16)
    return high, low


def gathered_tables(length, groups):
    rows = length // LANES
    coarse = np.arange(rows, dtype=np.float64)
    fine = np.arange(LANES, dtype=np.float64)
    phase = 2.0 * np.pi / rows * (coarse[:, None] + 0.25) * coarse[None, :]
    first = np.concatenate([np.cos(phase), -np.sin(phase)])
    high, low = (part.reshape(2 * rows, groups, -1) for part in split_table(first))
    stage_first = np.concatenate([high, high, low, low], axis=2).reshape(2 * rows, 4 * rows)
    last = (first.T / length).reshape(groups, rows // groups, 2 * rows)
    turn = 2.0 * np.pi / length * (coarse[:, None] + 0.25) * fine[None, :]
    twiddle = np.stack([np.cos(turn), np.sin(turn)]).astype(np.float32)
    angle = 2.0 * np.pi / LANES * fine[:, None] * fine[None, :]
    cos, sin = np.cos(angle), np.sin(angle)
    second = np.block([[cos, -sin], [sin, cos]])
    return stage_first, twiddle, np.stack(split_table(second)), np.stack(split_table(last), axis=1)


def split(value):
    high = value.astype(jnp.bfloat16)
    return high, (value - high.astype(jnp.float32)).astype(jnp.bfloat16)


def dot(left, right):
    return jnp.dot(left, right, preferred_element_type=jnp.float32)


def product(left, right):
    return dot(left[0], right[0]) + dot(left[0], right[1]) + dot(left[1], right[0])


def stage_rows(block, channels):
    cells = block.shape[0] // 3
    pieces = []
    for channel in range(channels):
        for array in range(3):
            pieces.append(block[pl.ds(array * cells + channel, cells // channels, stride=channels)])
    value = jnp.concatenate(pieces, axis=1)
    high, low = split(value)
    return jnp.concatenate([high, low, high, low])


def stage_columns(table, group):
    width = table.shape[1] // lax.axis_size("seq")
    return table[:, pl.ds(pl.multiple_of(group * width, width), width)]


def own_kernel(channels, block, first, twiddle, second, last, out_ref):
    out_ref[...] = dot(stage_columns(first, lax.axis_index("seq")), stage_rows(block, channels))


def gathered_kernel(groups, channels, skip_ref, coarse_ref, *refs):
    blocks = refs[:groups]
    first, twiddle, second, last = refs[groups : groups + 4]
    grad_signal_ref, grad_filter_ref, grad_skip_ref = refs[groups + 4 :]
    device = lax.axis_index("seq")
    rows = twiddle.shape[1]
    height = rows // groups

    columns = [stage_columns(first, lax.bitwise_xor(device, step)) for step in range(1, groups)]
    data = [stage_rows(block, channels) for block in blocks[1:]]
    coarse = coarse_ref[...] + dot(jnp.concatenate(columns, axis=1), jnp.concatenate(data))
    cos, sin = twiddle[0], twiddle[1]
    turned = []
    for index in range(3 * channels):
        lanes = slice(index * LANES, (index + 1) * LANES)
        real, imag = coarse[:rows, lanes], coarse[rows:, lanes]
        turned.append(jnp.concatenate([real * cos + imag * sin, imag * cos - real * sin], axis=1))
    spectra = product(split(jnp.concatenate(turned)), (second[0], second[1]))
    products = []
    for channel in range(channels):
        grad = spectra[(3 * channel + 2) * rows : (3 * channel + 3) * rows]
        grad_real, grad_imag = grad[:, :LANES], grad[:, LANES:]
        for array in range(2):
            other = spectra[(3 * channel + array) * rows : (3 * channel + array + 1) * rows]
            real, imag = other[:, :LANES], other[:, LANES:]
            products.append(
                jnp.concatenate([real * grad_real + imag * grad_imag, imag * grad_real - real * grad_imag], axis=1)
            )
    back = product(split(jnp.concatenate(products)), (second[0], second[1]))
    spread = []
    for index in range(2 * channels):
        value = back[index * rows : (index + 1) * rows]
        real, minus = value[:, :LANES], value[:, LANES:]
        spread.append(jnp.concatenate([real * cos + minus * sin, real * sin - minus * cos]))
    result = product((last[device, 0], last[device, 1]), split(jnp.concatenate(spread, axis=1)))

    cells = height * channels
    total = sum(block[cells : 2 * cells] * block[2 * cells :] for block in blocks)
    owner = lax.broadcasted_iota(jnp.int32, total.shape, 0) % channels
    for channel in range(channels):
        grad_skip_ref[channel] = jnp.sum(jnp.where(owner == channel, total, 0.0))
        mine = pl.ds(channel, height, stride=channels)
        lanes = 2 * channel * LANES
        kept = skip_ref[channel] * blocks[0][pl.ds(2 * cells + channel, height, stride=channels)]
        grad_signal_ref[mine, :] = result[:, lanes : lanes + LANES] + kept
        grad_filter_ref[mine, :] = result[:, lanes + LANES : lanes + 2 * LANES]


def dense(value):
    channels, cells = value.shape
    return value.reshape(channels, cells // LANES, LANES).transpose(1, 0, 2).reshape(-1, LANES)


def undense(value, channels):
    return value.reshape(-1, channels, LANES).transpose(1, 0, 2).reshape(channels, -1)


def gathered_body(signal, filter_taps, grad_out, skip):
    groups = lax.axis_size("seq")
    channels, cells = signal.shape
    length = cells * groups
    rows = length // LANES
    own = jnp.concatenate([dense(filter_taps), dense(signal), dense(grad_out)])
    blocks = [own]
    for step in range(1, groups):
        blocks.append(lax.ppermute(own, "seq", [(index, index ^ step) for index in range(groups)]))
    tables = [jnp.asarray(table) for table in gathered_tables(length, groups)]
    whole = pl.BlockSpec(memory_space=pltpu.VMEM)
    scalar = pl.BlockSpec(memory_space=pltpu.SMEM)
    params = pltpu.CompilerParams(vmem_limit_bytes=24 * 2**20)
    coarse = pl.pallas_call(
        functools.partial(own_kernel, channels),
        out_shape=jax.ShapeDtypeStruct((2 * rows, 3 * channels * LANES), jnp.float32),
        in_specs=[whole] * 5,
        out_specs=whole,
        compiler_params=params,
        cost_estimate=pl.CostEstimate(flops=2**27, bytes_accessed=2**21, transcendentals=0),
        name="own_part",
    )(own, *tables)
    shape = jax.ShapeDtypeStruct(dense(signal).shape, jnp.float32)
    grad_signal, grad_filter, grad_skip = pl.pallas_call(
        functools.partial(gathered_kernel, groups, channels),
        out_shape=(shape, shape, jax.ShapeDtypeStruct((channels,), jnp.float32)),
        in_specs=[scalar] + [whole] * (groups + 5),
        out_specs=(whole, whole, scalar),
        compiler_params=params,
        name="correlate",
    )(skip, coarse, *blocks, *tables)
    return (undense(grad_signal, channels), undense(grad_filter, channels), grad_skip)


def frequency_order(groups):
    slots = jnp.arange(2 * groups, dtype=jnp.int32)
    halves = slots // 2
    return jnp.where(slots % 2 == 0, halves, jnp.where(halves == 0, groups, 2 * groups - halves))


def phase_table(left_index, right_index, period):
    product = left_index[:, None] * right_index[None, :] % period
    return 2.0 * math.pi / period * product.astype(jnp.float32)


def transform_tables(cells):
    inner_len = 128
    outer_len = cells // inner_len
    outer_range = jnp.arange(outer_len, dtype=jnp.int32)
    inner_range = jnp.arange(inner_len, dtype=jnp.int32)
    outer_phase = phase_table(outer_range, outer_range, outer_len)
    twist_phase = phase_table(outer_range, inner_range, cells)
    inner_phase = phase_table(inner_range, inner_range, inner_len)
    return (
        jnp.cos(outer_phase),
        jnp.sin(outer_phase),
        jnp.cos(twist_phase),
        jnp.sin(twist_phase),
        jnp.cos(inner_phase),
        jnp.sin(inner_phase),
    )


def complex_apply(real_part, imag_part, cos_table, sin_table, pattern, turning):
    first = jnp.einsum(pattern, real_part, cos_table, precision=highest) - turning * jnp.einsum(
        pattern, imag_part, sin_table, precision=highest
    )
    second = jnp.einsum(pattern, imag_part, cos_table, precision=highest) + turning * jnp.einsum(
        pattern, real_part, sin_table, precision=highest
    )
    return (first, second)


def forward_transform(real_part, imag_part, tables):
    outer_cos, outer_sin, twist_cos, twist_sin, inner_cos, inner_sin = tables
    outer_len = outer_cos.shape[0]
    inner_len = inner_cos.shape[0]
    initial = real_part.shape
    folded = initial[:-1] + (outer_len, inner_len)
    real_part = real_part.reshape(folded)
    imag_part = imag_part.reshape(folded)
    real_part, imag_part = complex_apply(
        real_part, imag_part, outer_cos, outer_sin, "...ab,ac->...cb", -1.0
    )
    real_part, imag_part = (
        real_part * twist_cos + imag_part * twist_sin,
        imag_part * twist_cos - real_part * twist_sin,
    )
    real_part, imag_part = complex_apply(
        real_part, imag_part, inner_cos, inner_sin, "...cb,bd->...cd", -1.0
    )
    return (real_part.reshape(initial), imag_part.reshape(initial))


def inverse_transform(real_part, imag_part, tables):
    outer_cos, outer_sin, twist_cos, twist_sin, inner_cos, inner_sin = tables
    outer_len = outer_cos.shape[0]
    inner_len = inner_cos.shape[0]
    initial = real_part.shape
    folded = initial[:-1] + (outer_len, inner_len)
    real_part = real_part.reshape(folded)
    imag_part = imag_part.reshape(folded)
    real_part, imag_part = complex_apply(
        real_part, imag_part, inner_cos, inner_sin, "...cd,bd->...cb", 1.0
    )
    real_part, imag_part = (
        real_part * twist_cos - imag_part * twist_sin,
        imag_part * twist_cos + real_part * twist_sin,
    )
    real_part, imag_part = complex_apply(
        real_part, imag_part, outer_cos, outer_sin, "...cb,ac->...ab", 1.0
    )
    return (real_part.reshape(initial), imag_part.reshape(initial))


def split_body(signal, filter_taps, grad_out, skip):
    groups = lax.axis_size("seq")
    device = lax.axis_index("seq")
    cells = signal.shape[1]
    width = cells // groups
    doubled = 2 * groups
    period = doubled * cells
    freq_slots = frequency_order(groups)
    tables = transform_tables(cells)
    stacked = jnp.stack([signal, filter_taps, grad_out])[:, :, None, :]
    columns = lax.all_to_all(stacked, "seq", split_axis=3, concat_axis=2, tiled=True)
    group_rows = jnp.arange(groups, dtype=jnp.int32)
    group_phase = phase_table(group_rows, freq_slots, doubled)
    group_cos = jnp.cos(group_phase)
    group_sin = jnp.sin(group_phase)
    real_part = jnp.einsum("acpj,pm->acmj", columns, group_cos, precision=highest)
    imag_part = -jnp.einsum("acpj,pm->acmj", columns, group_sin, precision=highest)
    residues = device * width + jnp.arange(width, dtype=jnp.int32)
    twist_phase = phase_table(freq_slots, residues, period)
    twist_cos = jnp.cos(twist_phase)
    twist_sin = jnp.sin(twist_phase)
    twisted_real = real_part * twist_cos + imag_part * twist_sin
    twisted_imag = imag_part * twist_cos - real_part * twist_sin
    outgoing = jnp.stack([twisted_real, twisted_imag], 1)
    spectra = lax.all_to_all(outgoing, "seq", split_axis=3, concat_axis=4, tiled=True)
    freq_real, freq_imag = forward_transform(spectra[:, 0], spectra[:, 1], tables)
    grad_real = freq_real[-1]
    grad_imag = freq_imag[-1]
    signal_real, signal_imag = (freq_real[0], freq_imag[0])
    filter_real, filter_imag = (freq_real[1], freq_imag[1])
    input_real = filter_real * grad_real + filter_imag * grad_imag
    input_imag = filter_real * grad_imag - filter_imag * grad_real
    taps_real = signal_real * grad_real + signal_imag * grad_imag
    taps_imag = signal_real * grad_imag - signal_imag * grad_real
    back_real = jnp.stack([input_real, taps_real])
    back_imag = jnp.stack([input_imag, taps_imag])
    inverse_real, inverse_imag = inverse_transform(back_real, back_imag, tables)
    full_range = jnp.arange(cells, dtype=jnp.int32)
    local_slots = lax.dynamic_slice_in_dim(freq_slots, 2 * device, 2)
    back_phase = phase_table(local_slots, full_range, period)
    back_cos = jnp.cos(back_phase)
    back_sin = jnp.sin(back_phase)
    turned_real = inverse_real * back_cos - inverse_imag * back_sin
    turned_imag = inverse_imag * back_cos + inverse_real * back_sin
    returning = jnp.stack([turned_real, turned_imag], 1)
    residue_rows = lax.all_to_all(returning, "seq", split_axis=4, concat_axis=3, tiled=True)
    scale = 1.0 / period
    real_out = (
        jnp.einsum("ncmj,pm->ncpj", residue_rows[:, 0], group_cos, precision=highest)
        - jnp.einsum("ncmj,pm->ncpj", residue_rows[:, 1], group_sin, precision=highest)
    ) * scale
    gathered = lax.all_to_all(real_out, "seq", split_axis=2, concat_axis=3, tiled=True)
    grad_signal = gathered[0, :, 0, :] + skip[:, None] * grad_out
    grad_filter = gathered[1, :, 0, :]
    grad_skip = lax.psum(jnp.sum(grad_out * signal, axis=1), "seq")
    return (grad_signal, grad_filter, grad_skip)


def body(signal, filter_taps, grad_out, skip):
    groups = lax.axis_size("seq")
    channels, cells = signal.shape
    whole_fits = channels * cells * groups <= 2**15
    if whole_fits and groups & (groups - 1) == 0 and cells % (16 * LANES) == 0:
        return gathered_body(signal, filter_taps, grad_out, skip)
    return split_body(signal, filter_taps, grad_out, skip)
def solution(mesh):
    return jax.shard_map(
        body,
        mesh=mesh,
        in_specs=(
            P(("parts", "chan", "sub"), "seq"),
            P(("parts", "chan", "sub"), "seq"),
            P(("parts", "chan", "sub"), "seq"),
            P(("parts", "chan", "sub")),
        ),
        out_specs=(
            P(("parts", "chan", "sub"), "seq"),
            P(("parts", "chan", "sub"), "seq"),
            P(("parts", "chan", "sub")),
        ),
        check_vma=False,
    )
```

```python
import functools
import math

import jax
import jax.numpy as jnp
import ml_dtypes
import numpy as np
from jax import lax
from jax.experimental import pallas as pl
from jax.experimental.pallas import tpu as pltpu
from jax.sharding import PartitionSpec as P

LANES = 128
highest = lax.Precision.HIGHEST


def split_table(table):
    high = table.astype(np.float32).astype(ml_dtypes.bfloat16)
    low = (table - high.astype(np.float64)).astype(np.float32).astype(ml_dtypes.bfloat16)
    return high, low


def gathered_tables(length, groups):
    rows = length // LANES
    coarse = np.arange(rows, dtype=np.float64)
    fine = np.arange(LANES, dtype=np.float64)
    phase = 2.0 * np.pi / rows * (coarse[:, None] + 0.25) * coarse[None, :]
    first = np.concatenate([np.cos(phase), -np.sin(phase)])
    high, low = (part.reshape(2 * rows, groups, -1) for part in split_table(first))
    stage_first = np.concatenate([high, high, low, low], axis=2).reshape(2 * rows, 4 * rows)
    last = (first.T / length).reshape(groups, rows // groups, 2 * rows)
    turn = 2.0 * np.pi / length * (coarse[:, None] + 0.25) * fine[None, :]
    twiddle = np.stack([np.cos(turn), np.sin(turn)]).astype(np.float32)
    angle = 2.0 * np.pi / LANES * fine[:, None] * fine[None, :]
    cos, sin = np.cos(angle), np.sin(angle)
    second = np.block([[cos, -sin], [sin, cos]])
    return stage_first, twiddle, np.stack(split_table(second)), np.stack(split_table(last), axis=1)


def split(value):
    high = value.astype(jnp.bfloat16)
    return high, (value - high.astype(jnp.float32)).astype(jnp.bfloat16)


def dot(left, right):
    return jnp.dot(left, right, preferred_element_type=jnp.float32)


def product(left, right):
    return dot(jnp.concatenate([left[0], left[0], left[1]], axis=1), jnp.concatenate([right[0], right[1], right[0]]))


def stage_rows(block, channels):
    cells = block.shape[0] // 3
    pieces = []
    for channel in range(channels):
        for array in range(3):
            pieces.append(block[pl.ds(array * cells + channel, cells // channels, stride=channels)])
    value = jnp.concatenate(pieces, axis=1)
    high, low = split(value)
    return jnp.concatenate([high, low, high, low])


def stage_columns(table, group):
    width = table.shape[1] // lax.axis_size("seq")
    return table[:, pl.ds(pl.multiple_of(group * width, width), width)]


def cycle_entry(index):
    return index ^ (index >> 1)


def sender(device, step, groups):
    place = device
    shift = 1
    while 1 << shift < groups:
        place = lax.bitwise_xor(place, lax.shift_right_logical(device, shift))
        shift += 1
    place = lax.rem(place + (groups - step), groups)
    return lax.bitwise_xor(place, lax.shift_right_logical(place, 1))


def own_kernel(channels, block, first, twiddle, second, last, out_ref):
    out_ref[...] = dot(stage_columns(first, lax.axis_index("seq")), stage_rows(block, channels))


def gathered_kernel(groups, channels, skip_ref, coarse_ref, *refs):
    blocks = refs[:groups]
    first, twiddle, second, last = refs[groups : groups + 4]
    grad_signal_ref, grad_filter_ref, grad_skip_ref = refs[groups + 4 :]
    skips = skip_ref[...]
    device = lax.axis_index("seq")
    rows = twiddle.shape[1]
    height = rows // groups

    senders = [sender(device, step, groups) for step in reversed(range(1, groups))]
    columns = jnp.concatenate([stage_columns(first, index) for index in senders], axis=1)
    cos, sin = twiddle[0], twiddle[1]
    data = jnp.concatenate([stage_rows(block, channels) for block in blocks[1:]])

    def stage1(channel):
        lanes = slice(3 * channel * LANES, 3 * (channel + 1) * LANES)
        return coarse_ref[:, lanes] + dot(columns, data[:, lanes])

    def turn_out(coarse):
        part = []
        for array in range(3):
            lanes = slice(array * LANES, (array + 1) * LANES)
            real, imag = coarse[:rows, lanes], coarse[rows:, lanes]
            part.append(jnp.concatenate([real * cos + imag * sin, imag * cos - real * sin], axis=1))
        return split(jnp.concatenate(part))

    def wide(value):
        return product(value, (second[0], second[1]))

    def mix(spectra):
        grad = spectra[2 * rows :]
        grad_real, grad_imag = grad[:, :LANES], grad[:, LANES:]
        part = []
        for array in range(2):
            other = spectra[array * rows : (array + 1) * rows]
            real, imag = other[:, :LANES], other[:, LANES:]
            part.append(
                jnp.concatenate([real * grad_real + imag * grad_imag, imag * grad_real - real * grad_imag], axis=1)
            )
        return split(jnp.concatenate(part))

    def turn_back(back):
        spread = []
        for array in range(2):
            value = back[array * rows : (array + 1) * rows]
            real, minus = value[:, :LANES], value[:, LANES:]
            spread.append(jnp.concatenate([real * cos + minus * sin, real * sin - minus * cos]))
        return split(jnp.concatenate(spread, axis=1))

    turned = [turn_out(stage1(channel)) for channel in range(channels)]
    spectra = [wide(value) for value in turned]
    mixed = [mix(value) for value in spectra]
    back = [wide(value) for value in mixed]
    spread = [turn_back(value) for value in back]
    result = jnp.concatenate([product((last[device, 0], last[device, 1]), value) for value in spread], axis=1)

    cells = height * channels
    total = sum(block[cells : 2 * cells] * block[2 * cells :] for block in blocks)
    owner = lax.broadcasted_iota(jnp.int32, total.shape, 0) % channels
    for channel in range(channels):
        grad_skip_ref[channel] = jnp.sum(jnp.where(owner == channel, total, 0.0))
        mine = pl.ds(channel, height, stride=channels)
        lanes = 2 * channel * LANES
        kept = skips[channel] * blocks[0][pl.ds(2 * cells + channel, height, stride=channels)]
        grad_signal_ref[mine, :] = result[:, lanes : lanes + LANES] + kept
        grad_filter_ref[mine, :] = result[:, lanes + LANES : lanes + 2 * LANES]


def dense(value):
    channels, cells = value.shape
    return value.reshape(channels, cells // LANES, LANES).transpose(1, 0, 2).reshape(-1, LANES)


def undense(value, channels):
    return value.reshape(-1, channels, LANES).transpose(1, 0, 2).reshape(channels, -1)


def gathered_body(signal, filter_taps, grad_out, skip):
    groups = lax.axis_size("seq")
    channels, cells = signal.shape
    length = cells * groups
    rows = length // LANES
    own = jnp.concatenate([dense(filter_taps), dense(signal), dense(grad_out)])
    blocks = [own]
    for step in reversed(range(1, groups)):
        hops = [(cycle_entry(index), cycle_entry((index + step) % groups)) for index in range(groups)]
        blocks.append(lax.ppermute(own, "seq", hops))
    tables = [jnp.asarray(table) for table in gathered_tables(length, groups)]
    whole = pl.BlockSpec(memory_space=pltpu.VMEM)
    scalar = pl.BlockSpec(memory_space=pltpu.SMEM)
    params = pltpu.CompilerParams(vmem_limit_bytes=24 * 2**20)
    coarse = pl.pallas_call(
        functools.partial(own_kernel, channels),
        out_shape=jax.ShapeDtypeStruct((2 * rows, 3 * channels * LANES), jnp.float32),
        in_specs=[whole] * 5,
        out_specs=whole,
        compiler_params=params,
        cost_estimate=pl.CostEstimate(flops=2**27, bytes_accessed=2**21, transcendentals=0),
        name="own_part",
    )(own, *tables)
    shape = jax.ShapeDtypeStruct(dense(signal).shape, jnp.float32)
    grad_signal, grad_filter, grad_skip = pl.pallas_call(
        functools.partial(gathered_kernel, groups, channels),
        out_shape=(shape, shape, jax.ShapeDtypeStruct((channels,), jnp.float32)),
        in_specs=[whole] + [whole] * (groups + 5),
        out_specs=(whole, whole, scalar),
        compiler_params=params,
        name="correlate",
    )(skip, coarse, *blocks, *tables)
    return (undense(grad_signal, channels), undense(grad_filter, channels), grad_skip)


def frequency_order(groups):
    slots = jnp.arange(2 * groups, dtype=jnp.int32)
    halves = slots // 2
    return jnp.where(slots % 2 == 0, halves, jnp.where(halves == 0, groups, 2 * groups - halves))


def phase_table(left_index, right_index, period):
    product = left_index[:, None] * right_index[None, :] % period
    return 2.0 * math.pi / period * product.astype(jnp.float32)


def transform_tables(cells):
    inner_len = 128
    outer_len = cells // inner_len
    outer_range = jnp.arange(outer_len, dtype=jnp.int32)
    inner_range = jnp.arange(inner_len, dtype=jnp.int32)
    outer_phase = phase_table(outer_range, outer_range, outer_len)
    twist_phase = phase_table(outer_range, inner_range, cells)
    inner_phase = phase_table(inner_range, inner_range, inner_len)
    return (
        jnp.cos(outer_phase),
        jnp.sin(outer_phase),
        jnp.cos(twist_phase),
        jnp.sin(twist_phase),
        jnp.cos(inner_phase),
        jnp.sin(inner_phase),
    )


def complex_apply(real_part, imag_part, cos_table, sin_table, pattern, turning):
    first = jnp.einsum(pattern, real_part, cos_table, precision=highest) - turning * jnp.einsum(
        pattern, imag_part, sin_table, precision=highest
    )
    second = jnp.einsum(pattern, imag_part, cos_table, precision=highest) + turning * jnp.einsum(
        pattern, real_part, sin_table, precision=highest
    )
    return (first, second)


def forward_transform(real_part, imag_part, tables):
    outer_cos, outer_sin, twist_cos, twist_sin, inner_cos, inner_sin = tables
    outer_len = outer_cos.shape[0]
    inner_len = inner_cos.shape[0]
    initial = real_part.shape
    folded = initial[:-1] + (outer_len, inner_len)
    real_part = real_part.reshape(folded)
    imag_part = imag_part.reshape(folded)
    real_part, imag_part = complex_apply(
        real_part, imag_part, outer_cos, outer_sin, "...ab,ac->...cb", -1.0
    )
    real_part, imag_part = (
        real_part * twist_cos + imag_part * twist_sin,
        imag_part * twist_cos - real_part * twist_sin,
    )
    real_part, imag_part = complex_apply(
        real_part, imag_part, inner_cos, inner_sin, "...cb,bd->...cd", -1.0
    )
    return (real_part.reshape(initial), imag_part.reshape(initial))


def inverse_transform(real_part, imag_part, tables):
    outer_cos, outer_sin, twist_cos, twist_sin, inner_cos, inner_sin = tables
    outer_len = outer_cos.shape[0]
    inner_len = inner_cos.shape[0]
    initial = real_part.shape
    folded = initial[:-1] + (outer_len, inner_len)
    real_part = real_part.reshape(folded)
    imag_part = imag_part.reshape(folded)
    real_part, imag_part = complex_apply(
        real_part, imag_part, inner_cos, inner_sin, "...cd,bd->...cb", 1.0
    )
    real_part, imag_part = (
        real_part * twist_cos - imag_part * twist_sin,
        imag_part * twist_cos + real_part * twist_sin,
    )
    real_part, imag_part = complex_apply(
        real_part, imag_part, outer_cos, outer_sin, "...cb,ac->...ab", 1.0
    )
    return (real_part.reshape(initial), imag_part.reshape(initial))


def split_body(signal, filter_taps, grad_out, skip):
    groups = lax.axis_size("seq")
    device = lax.axis_index("seq")
    cells = signal.shape[1]
    width = cells // groups
    doubled = 2 * groups
    period = doubled * cells
    freq_slots = frequency_order(groups)
    tables = transform_tables(cells)
    stacked = jnp.stack([signal, filter_taps, grad_out])[:, :, None, :]
    columns = lax.all_to_all(stacked, "seq", split_axis=3, concat_axis=2, tiled=True)
    group_rows = jnp.arange(groups, dtype=jnp.int32)
    group_phase = phase_table(group_rows, freq_slots, doubled)
    group_cos = jnp.cos(group_phase)
    group_sin = jnp.sin(group_phase)
    real_part = jnp.einsum("acpj,pm->acmj", columns, group_cos, precision=highest)
    imag_part = -jnp.einsum("acpj,pm->acmj", columns, group_sin, precision=highest)
    residues = device * width + jnp.arange(width, dtype=jnp.int32)
    twist_phase = phase_table(freq_slots, residues, period)
    twist_cos = jnp.cos(twist_phase)
    twist_sin = jnp.sin(twist_phase)
    twisted_real = real_part * twist_cos + imag_part * twist_sin
    twisted_imag = imag_part * twist_cos - real_part * twist_sin
    outgoing = jnp.stack([twisted_real, twisted_imag], 1)
    spectra = lax.all_to_all(outgoing, "seq", split_axis=3, concat_axis=4, tiled=True)
    freq_real, freq_imag = forward_transform(spectra[:, 0], spectra[:, 1], tables)
    grad_real = freq_real[-1]
    grad_imag = freq_imag[-1]
    signal_real, signal_imag = (freq_real[0], freq_imag[0])
    filter_real, filter_imag = (freq_real[1], freq_imag[1])
    input_real = filter_real * grad_real + filter_imag * grad_imag
    input_imag = filter_real * grad_imag - filter_imag * grad_real
    taps_real = signal_real * grad_real + signal_imag * grad_imag
    taps_imag = signal_real * grad_imag - signal_imag * grad_real
    back_real = jnp.stack([input_real, taps_real])
    back_imag = jnp.stack([input_imag, taps_imag])
    inverse_real, inverse_imag = inverse_transform(back_real, back_imag, tables)
    full_range = jnp.arange(cells, dtype=jnp.int32)
    local_slots = lax.dynamic_slice_in_dim(freq_slots, 2 * device, 2)
    back_phase = phase_table(local_slots, full_range, period)
    back_cos = jnp.cos(back_phase)
    back_sin = jnp.sin(back_phase)
    turned_real = inverse_real * back_cos - inverse_imag * back_sin
    turned_imag = inverse_imag * back_cos + inverse_real * back_sin
    returning = jnp.stack([turned_real, turned_imag], 1)
    residue_rows = lax.all_to_all(returning, "seq", split_axis=4, concat_axis=3, tiled=True)
    scale = 1.0 / period
    real_out = (
        jnp.einsum("ncmj,pm->ncpj", residue_rows[:, 0], group_cos, precision=highest)
        - jnp.einsum("ncmj,pm->ncpj", residue_rows[:, 1], group_sin, precision=highest)
    ) * scale
    gathered = lax.all_to_all(real_out, "seq", split_axis=2, concat_axis=3, tiled=True)
    grad_signal = gathered[0, :, 0, :] + skip[:, None] * grad_out
    grad_filter = gathered[1, :, 0, :]
    grad_skip = lax.psum(jnp.sum(grad_out * signal, axis=1), "seq")
    return (grad_signal, grad_filter, grad_skip)


def body(signal, filter_taps, grad_out, skip):
    groups = lax.axis_size("seq")
    channels, cells = signal.shape
    whole_fits = channels * cells * groups <= 2**15
    if whole_fits and groups & (groups - 1) == 0 and cells % (16 * LANES) == 0:
        return gathered_body(signal, filter_taps, grad_out, skip)
    return split_body(signal, filter_taps, grad_out, skip)
def solution(mesh):
    return jax.shard_map(
        body,
        mesh=mesh,
        in_specs=(
            P(("parts", "chan", "sub"), "seq"),
            P(("parts", "chan", "sub"), "seq"),
            P(("parts", "chan", "sub"), "seq"),
            P(("parts", "chan", "sub")),
        ),
        out_specs=(
            P(("parts", "chan", "sub"), "seq"),
            P(("parts", "chan", "sub"), "seq"),
            P(("parts", "chan", "sub")),
        ),
        check_vma=False,
    )
```

```python
import functools
import math

import jax
import jax.numpy as jnp
import ml_dtypes
import numpy as np
from jax import lax
from jax.experimental import pallas as pl
from jax.experimental.pallas import tpu as pltpu
from jax.sharding import PartitionSpec as P

LANES = 128
highest = lax.Precision.HIGHEST


def split_table(table):
    high = table.astype(np.float32).astype(ml_dtypes.bfloat16)
    low = (table - high.astype(np.float64)).astype(np.float32).astype(ml_dtypes.bfloat16)
    return high, low


def gathered_tables(length, groups):
    rows = length // LANES
    coarse = np.arange(rows, dtype=np.float64)
    fine = np.arange(LANES, dtype=np.float64)
    phase = 2.0 * np.pi / rows * (coarse[:, None] + 0.25) * coarse[None, :]
    first = np.concatenate([np.cos(phase), -np.sin(phase)])
    high, low = (part.reshape(2 * rows, groups, -1) for part in split_table(first))
    stage_first = np.concatenate([high, high, low, low], axis=2).reshape(2 * rows, 4 * rows)
    last = (first.T / length).reshape(groups, rows // groups, 2 * rows)
    turn = 2.0 * np.pi / length * (coarse[:, None] + 0.25) * fine[None, :]
    twiddle = np.stack([np.cos(turn), np.sin(turn)]).astype(np.float32)
    angle = 2.0 * np.pi / LANES * fine[:, None] * fine[None, :]
    cos, sin = np.cos(angle), np.sin(angle)
    second = np.block([[cos, -sin], [sin, cos]])
    return stage_first, twiddle, np.stack(split_table(second)), np.concatenate(split_table(last), axis=1)


def split(value):
    high = value.astype(jnp.bfloat16)
    return high, (value - high.astype(jnp.float32)).astype(jnp.bfloat16)


def dot(left, right):
    return jnp.dot(left, right, preferred_element_type=jnp.float32)


def product(left, right):
    return dot(jnp.concatenate([left[0], left[0], left[1]], axis=1), jnp.concatenate([right[0], right[1], right[0]]))


def stage_rows(block, channels):
    cells = block.shape[0] // 3
    pieces = []
    for channel in range(channels):
        for array in range(3):
            pieces.append(block[pl.ds(array * cells + channel, cells // channels, stride=channels)])
    value = jnp.concatenate(pieces, axis=1)
    high, low = split(value)
    return jnp.concatenate([high, low, high, low])


def stage_columns(table, group):
    width = table.shape[1] // lax.axis_size("seq")
    return table[:, pl.ds(pl.multiple_of(group * width, width), width)]


def routes(groups, cores):
    plans = [(tuple(range(groups)), tuple(range(1, groups)))]
    if groups == 4:
        plans = [((0, 2, 1, 3), (3, 1, 2)), ((0, 1, 3, 2), (1, 2, 3))]
    steps = []
    for index in range(groups - 1):
        targets = []
        for core in range(cores):
            cycle, moves = plans[core % len(plans)]
            ahead = {cycle[place]: cycle[(place + moves[index]) % groups] for place in range(groups)}
            targets.append([ahead[device] for device in range(groups)])
        steps.append(targets)
    return steps


def sender(targets):
    code = 0
    for core, ahead in enumerate(targets):
        packed = sum(device << 4 * target for device, target in enumerate(ahead))
        code = jnp.where(lax.axis_index("sub") == core, packed, code)
    return lax.bitwise_and(lax.shift_right_logical(code, 4 * lax.axis_index("seq")), 15)


def own_kernel(channels, block, first, twiddle, second, last, out_ref):
    out_ref[...] = dot(stage_columns(first, lax.axis_index("seq")), stage_rows(block, channels))


def early_kernel(channels, targets, coarse_ref, block, first, out_ref):
    out_ref[...] = coarse_ref[...] + dot(stage_columns(first, sender(targets)), stage_rows(block, channels))


def gathered_kernel(groups, channels, late, skip_ref, coarse_ref, *refs):
    blocks = refs[:groups]
    first, twiddle, second, last = refs[groups : groups + 4]
    grad_signal_ref, grad_filter_ref, grad_skip_ref = refs[groups + 4 :]
    skips = skip_ref[...]
    device = lax.axis_index("seq")
    rows = twiddle.shape[1]
    height = rows // groups

    columns = jnp.concatenate([stage_columns(first, sender(targets)) for targets in late], axis=1)
    data = jnp.concatenate([stage_rows(block, channels) for block in blocks[groups - len(late) :]])
    cos, sin = twiddle[0], twiddle[1]
    last_rows = last[device]

    def stage1(channel):
        lanes = slice(3 * channel * LANES, 3 * (channel + 1) * LANES)
        return coarse_ref[:, lanes] + dot(columns, data[:, lanes])

    def turn_out(coarse):
        part = []
        for array in range(3):
            lanes = slice(array * LANES, (array + 1) * LANES)
            real, imag = coarse[:rows, lanes], coarse[rows:, lanes]
            part.append(jnp.concatenate([real * cos + imag * sin, imag * cos - real * sin], axis=1))
        return split(jnp.concatenate(part))

    def wide(value):
        return product(value, (second[0], second[1]))

    def mix(spectra):
        grad = spectra[2 * rows :]
        grad_real, grad_imag = grad[:, :LANES], grad[:, LANES:]
        part = []
        for array in range(2):
            other = spectra[array * rows : (array + 1) * rows]
            real, imag = other[:, :LANES], other[:, LANES:]
            part.append(
                jnp.concatenate([real * grad_real + imag * grad_imag, imag * grad_real - real * grad_imag], axis=1)
            )
        return split(jnp.concatenate(part))

    def turn_back(back):
        spread = []
        for array in range(2):
            value = back[array * rows : (array + 1) * rows]
            real, minus = value[:, :LANES], value[:, LANES:]
            spread.append(jnp.concatenate([real * cos + minus * sin, real * sin - minus * cos]))
        return split(jnp.concatenate(spread, axis=1))

    def narrow(value):
        both = dot(last_rows, value[0])
        return both[:height] + both[height:] + dot(last_rows[:height], value[1])

    turned = [turn_out(stage1(channel)) for channel in range(channels)]
    spectra = [wide(value) for value in turned]
    mixed = [mix(value) for value in spectra]
    back = [wide(value) for value in mixed]
    spread = [turn_back(value) for value in back]
    result = jnp.concatenate([narrow(value) for value in spread], axis=1)

    cells = height * channels
    total = sum(block[cells : 2 * cells] * block[2 * cells :] for block in blocks)
    owner = lax.broadcasted_iota(jnp.int32, total.shape, 0) % channels
    for channel in range(channels):
        grad_skip_ref[channel] = jnp.sum(jnp.where(owner == channel, total, 0.0))
        mine = pl.ds(channel, height, stride=channels)
        lanes = 2 * channel * LANES
        kept = skips[channel] * blocks[0][pl.ds(2 * cells + channel, height, stride=channels)]
        grad_signal_ref[mine, :] = result[:, lanes : lanes + LANES] + kept
        grad_filter_ref[mine, :] = result[:, lanes + LANES : lanes + 2 * LANES]


def dense(value):
    channels, cells = value.shape
    return value.reshape(channels, cells // LANES, LANES).transpose(1, 0, 2).reshape(-1, LANES)


def undense(value, channels):
    return value.reshape(-1, channels, LANES).transpose(1, 0, 2).reshape(channels, -1)


def gathered_body(signal, filter_taps, grad_out, skip):
    groups = lax.axis_size("seq")
    channels, cells = signal.shape
    length = cells * groups
    rows = length // LANES
    own = jnp.concatenate([dense(filter_taps), dense(signal), dense(grad_out)])
    cores = lax.axis_size("sub")
    steps = routes(groups, cores)
    arrived = []
    for targets in reversed(steps):
        hops = []
        for core, ahead in enumerate(targets):
            hops += [(device * cores + core, target * cores + core) for device, target in enumerate(ahead)]
        arrived.insert(0, lax.ppermute(own, ("seq", "sub"), hops))
    tables = [jnp.asarray(table) for table in gathered_tables(length, groups)]
    whole = pl.BlockSpec(memory_space=pltpu.VMEM)
    scalar = pl.BlockSpec(memory_space=pltpu.SMEM)
    params = pltpu.CompilerParams(vmem_limit_bytes=24 * 2**20)
    coarse = pl.pallas_call(
        functools.partial(own_kernel, channels),
        out_shape=jax.ShapeDtypeStruct((2 * rows, 3 * channels * LANES), jnp.float32),
        in_specs=[whole] * 5,
        out_specs=whole,
        compiler_params=params,
        cost_estimate=pl.CostEstimate(flops=2**27, bytes_accessed=2**21, transcendentals=0),
        name="own_part",
    )(own, *tables)
    coarse = pl.pallas_call(
        functools.partial(early_kernel, channels, steps[0]),
        out_shape=jax.ShapeDtypeStruct(coarse.shape, jnp.float32),
        in_specs=[whole] * 3,
        out_specs=whole,
        compiler_params=params,
        cost_estimate=pl.CostEstimate(flops=2**27, bytes_accessed=2**21, transcendentals=0),
        name="early_part",
    )(coarse, arrived[0], tables[0])
    shape = jax.ShapeDtypeStruct(dense(signal).shape, jnp.float32)
    grad_signal, grad_filter, grad_skip = pl.pallas_call(
        functools.partial(gathered_kernel, groups, channels, steps[1:]),
        out_shape=(shape, shape, jax.ShapeDtypeStruct((channels,), jnp.float32)),
        in_specs=[whole] + [whole] * (groups + 5),
        out_specs=(whole, whole, scalar),
        compiler_params=params,
        name="correlate",
    )(skip, coarse, own, *arrived, *tables)
    return (undense(grad_signal, channels), undense(grad_filter, channels), grad_skip)


def frequency_order(groups):
    slots = jnp.arange(2 * groups, dtype=jnp.int32)
    halves = slots // 2
    return jnp.where(slots % 2 == 0, halves, jnp.where(halves == 0, groups, 2 * groups - halves))


def phase_table(left_index, right_index, period):
    product = left_index[:, None] * right_index[None, :] % period
    return 2.0 * math.pi / period * product.astype(jnp.float32)


def transform_tables(cells):
    inner_len = 128
    outer_len = cells // inner_len
    outer_range = jnp.arange(outer_len, dtype=jnp.int32)
    inner_range = jnp.arange(inner_len, dtype=jnp.int32)
    outer_phase = phase_table(outer_range, outer_range, outer_len)
    twist_phase = phase_table(outer_range, inner_range, cells)
    inner_phase = phase_table(inner_range, inner_range, inner_len)
    return (
        jnp.cos(outer_phase),
        jnp.sin(outer_phase),
        jnp.cos(twist_phase),
        jnp.sin(twist_phase),
        jnp.cos(inner_phase),
        jnp.sin(inner_phase),
    )


def complex_apply(real_part, imag_part, cos_table, sin_table, pattern, turning):
    first = jnp.einsum(pattern, real_part, cos_table, precision=highest) - turning * jnp.einsum(
        pattern, imag_part, sin_table, precision=highest
    )
    second = jnp.einsum(pattern, imag_part, cos_table, precision=highest) + turning * jnp.einsum(
        pattern, real_part, sin_table, precision=highest
    )
    return (first, second)


def forward_transform(real_part, imag_part, tables):
    outer_cos, outer_sin, twist_cos, twist_sin, inner_cos, inner_sin = tables
    outer_len = outer_cos.shape[0]
    inner_len = inner_cos.shape[0]
    initial = real_part.shape
    folded = initial[:-1] + (outer_len, inner_len)
    real_part = real_part.reshape(folded)
    imag_part = imag_part.reshape(folded)
    real_part, imag_part = complex_apply(
        real_part, imag_part, outer_cos, outer_sin, "...ab,ac->...cb", -1.0
    )
    real_part, imag_part = (
        real_part * twist_cos + imag_part * twist_sin,
        imag_part * twist_cos - real_part * twist_sin,
    )
    real_part, imag_part = complex_apply(
        real_part, imag_part, inner_cos, inner_sin, "...cb,bd->...cd", -1.0
    )
    return (real_part.reshape(initial), imag_part.reshape(initial))


def inverse_transform(real_part, imag_part, tables):
    outer_cos, outer_sin, twist_cos, twist_sin, inner_cos, inner_sin = tables
    outer_len = outer_cos.shape[0]
    inner_len = inner_cos.shape[0]
    initial = real_part.shape
    folded = initial[:-1] + (outer_len, inner_len)
    real_part = real_part.reshape(folded)
    imag_part = imag_part.reshape(folded)
    real_part, imag_part = complex_apply(
        real_part, imag_part, inner_cos, inner_sin, "...cd,bd->...cb", 1.0
    )
    real_part, imag_part = (
        real_part * twist_cos - imag_part * twist_sin,
        imag_part * twist_cos + real_part * twist_sin,
    )
    real_part, imag_part = complex_apply(
        real_part, imag_part, outer_cos, outer_sin, "...cb,ac->...ab", 1.0
    )
    return (real_part.reshape(initial), imag_part.reshape(initial))


def split_body(signal, filter_taps, grad_out, skip):
    groups = lax.axis_size("seq")
    device = lax.axis_index("seq")
    cells = signal.shape[1]
    width = cells // groups
    doubled = 2 * groups
    period = doubled * cells
    freq_slots = frequency_order(groups)
    tables = transform_tables(cells)
    stacked = jnp.stack([signal, filter_taps, grad_out])[:, :, None, :]
    columns = lax.all_to_all(stacked, "seq", split_axis=3, concat_axis=2, tiled=True)
    group_rows = jnp.arange(groups, dtype=jnp.int32)
    group_phase = phase_table(group_rows, freq_slots, doubled)
    group_cos = jnp.cos(group_phase)
    group_sin = jnp.sin(group_phase)
    real_part = jnp.einsum("acpj,pm->acmj", columns, group_cos, precision=highest)
    imag_part = -jnp.einsum("acpj,pm->acmj", columns, group_sin, precision=highest)
    residues = device * width + jnp.arange(width, dtype=jnp.int32)
    twist_phase = phase_table(freq_slots, residues, period)
    twist_cos = jnp.cos(twist_phase)
    twist_sin = jnp.sin(twist_phase)
    twisted_real = real_part * twist_cos + imag_part * twist_sin
    twisted_imag = imag_part * twist_cos - real_part * twist_sin
    outgoing = jnp.stack([twisted_real, twisted_imag], 1)
    spectra = lax.all_to_all(outgoing, "seq", split_axis=3, concat_axis=4, tiled=True)
    freq_real, freq_imag = forward_transform(spectra[:, 0], spectra[:, 1], tables)
    grad_real = freq_real[-1]
    grad_imag = freq_imag[-1]
    signal_real, signal_imag = (freq_real[0], freq_imag[0])
    filter_real, filter_imag = (freq_real[1], freq_imag[1])
    input_real = filter_real * grad_real + filter_imag * grad_imag
    input_imag = filter_real * grad_imag - filter_imag * grad_real
    taps_real = signal_real * grad_real + signal_imag * grad_imag
    taps_imag = signal_real * grad_imag - signal_imag * grad_real
    back_real = jnp.stack([input_real, taps_real])
    back_imag = jnp.stack([input_imag, taps_imag])
    inverse_real, inverse_imag = inverse_transform(back_real, back_imag, tables)
    full_range = jnp.arange(cells, dtype=jnp.int32)
    local_slots = lax.dynamic_slice_in_dim(freq_slots, 2 * device, 2)
    back_phase = phase_table(local_slots, full_range, period)
    back_cos = jnp.cos(back_phase)
    back_sin = jnp.sin(back_phase)
    turned_real = inverse_real * back_cos - inverse_imag * back_sin
    turned_imag = inverse_imag * back_cos + inverse_real * back_sin
    returning = jnp.stack([turned_real, turned_imag], 1)
    residue_rows = lax.all_to_all(returning, "seq", split_axis=4, concat_axis=3, tiled=True)
    scale = 1.0 / period
    real_out = (
        jnp.einsum("ncmj,pm->ncpj", residue_rows[:, 0], group_cos, precision=highest)
        - jnp.einsum("ncmj,pm->ncpj", residue_rows[:, 1], group_sin, precision=highest)
    ) * scale
    gathered = lax.all_to_all(real_out, "seq", split_axis=2, concat_axis=3, tiled=True)
    grad_signal = gathered[0, :, 0, :] + skip[:, None] * grad_out
    grad_filter = gathered[1, :, 0, :]
    grad_skip = lax.psum(jnp.sum(grad_out * signal, axis=1), "seq")
    return (grad_signal, grad_filter, grad_skip)


def body(signal, filter_taps, grad_out, skip):
    groups = lax.axis_size("seq")
    channels, cells = signal.shape
    whole_fits = channels * cells * groups <= 2**15
    if whole_fits and groups <= 8 and cells % (16 * LANES) == 0:
        return gathered_body(signal, filter_taps, grad_out, skip)
    return split_body(signal, filter_taps, grad_out, skip)
def solution(mesh):
    return jax.shard_map(
        body,
        mesh=mesh,
        in_specs=(
            P(("parts", "chan", "sub"), "seq"),
            P(("parts", "chan", "sub"), "seq"),
            P(("parts", "chan", "sub"), "seq"),
            P(("parts", "chan", "sub")),
        ),
        out_specs=(
            P(("parts", "chan", "sub"), "seq"),
            P(("parts", "chan", "sub"), "seq"),
            P(("parts", "chan", "sub")),
        ),
        check_vma=False,
    )
```

```python
import functools
import itertools
import math

import jax
import jax.numpy as jnp
import ml_dtypes
import numpy as np
from jax import lax
from jax.experimental import pallas as pl
from jax.experimental.pallas import tpu as pltpu
from jax.sharding import PartitionSpec as P

LANES = 128
highest = lax.Precision.HIGHEST


def split_table(table):
    high = table.astype(np.float32).astype(ml_dtypes.bfloat16)
    low = (table - high.astype(np.float64)).astype(np.float32).astype(ml_dtypes.bfloat16)
    return high, low


def gathered_tables(length, groups):
    rows = length // LANES
    coarse = np.arange(rows, dtype=np.float64)
    fine = np.arange(LANES, dtype=np.float64)
    phase = 2.0 * np.pi / rows * (coarse[:, None] + 0.25) * coarse[None, :]
    first = np.concatenate([np.cos(phase), -np.sin(phase)])
    high, low = (part.reshape(2 * rows, groups, -1) for part in split_table(first))
    stage_first = np.concatenate([high, high, low, low], axis=2).reshape(2 * rows, 4 * rows)
    last = (first.T / length).reshape(groups, rows // groups, 2 * rows)
    turn = 2.0 * np.pi / length * (coarse[:, None] + 0.25) * fine[None, :]
    twiddle = np.stack([np.cos(turn), np.sin(turn)]).astype(np.float32)
    angle = 2.0 * np.pi / LANES * fine[:, None] * fine[None, :]
    cos, sin = np.cos(angle), np.sin(angle)
    second = np.block([[cos, -sin], [sin, cos]])
    return stage_first, twiddle, np.stack(split_table(second)), np.concatenate(split_table(last), axis=1)


def split(value):
    high = value.astype(jnp.bfloat16)
    return high, (value - high.astype(jnp.float32)).astype(jnp.bfloat16)


def dot(left, right):
    return jnp.dot(left, right, preferred_element_type=jnp.float32)


def product(left, right):
    rows = left[0].shape[0]
    both = dot(jnp.concatenate(left), right[0])
    return both[:rows] + both[rows:] + dot(left[0], right[1])


def stage_rows(block, channels):
    cells = block.shape[0] // 3
    pieces = []
    for channel in range(channels):
        for array in range(3):
            pieces.append(block[pl.ds(array * cells + channel, cells // channels, stride=channels)])
    value = jnp.concatenate(pieces, axis=1)
    high, low = split(value)
    return jnp.concatenate([high, low, high, low])


def stage_columns(table, group):
    width = table.shape[1] // lax.axis_size("seq")
    return table[:, pl.ds(pl.multiple_of(group * width, width), width)]


def routes(groups, cores):
    plain = (tuple(range(groups)), tuple(range(1, groups)))
    plans = [[plain], [plain]]
    if groups == 4:
        early, swift = ((0, 1, 3, 2), (1, 2, 3)), ((0, 2, 1, 3), (3, 1, 2))
        plans = [[swift, early], [early, swift]]
    steps = []
    for index in range(groups - 1):
        targets = []
        for line in plans:
            for core in range(cores):
                cycle, moves = line[core % len(line)]
                ahead = {cycle[place]: cycle[(place + moves[index]) % groups] for place in range(groups)}
                targets.append([ahead[device] for device in range(groups)])
        steps.append(targets)
    return steps


def sender(targets):
    line = jnp.where(lax.axis_index("parts") + lax.axis_index("chan") == 0, 0, 1)
    kind = line * lax.axis_size("sub") + lax.axis_index("sub")
    code = 0
    for index, ahead in enumerate(targets):
        packed = sum(device << 4 * target for device, target in enumerate(ahead))
        code = jnp.where(kind == index, packed, code)
    return lax.bitwise_and(lax.shift_right_logical(code, 4 * lax.axis_index("seq")), 15)


def own_kernel(channels, block, first, twiddle, second, last, out_ref):
    out_ref[...] = dot(stage_columns(first, lax.axis_index("seq")), stage_rows(block, channels))


def early_kernel(channels, targets, coarse_ref, block, first, out_ref):
    out_ref[...] = coarse_ref[...] + dot(stage_columns(first, sender(targets)), stage_rows(block, channels))


def gathered_kernel(groups, channels, late, skip_ref, coarse_ref, *refs):
    blocks = refs[:groups]
    first, twiddle, second, last = refs[groups : groups + 4]
    grad_signal_ref, grad_filter_ref, grad_skip_ref = refs[groups + 4 :]
    skips = skip_ref[...]
    device = lax.axis_index("seq")
    rows = twiddle.shape[1]
    height = rows // groups

    columns = jnp.concatenate([stage_columns(first, sender(targets)) for targets in late], axis=1)
    data = jnp.concatenate([stage_rows(block, channels) for block in blocks[groups - len(late) :]])
    cos, sin = twiddle[0], twiddle[1]
    last_rows = last[device]

    coarse = coarse_ref[...] + dot(columns, data)

    def turn_out(coarse):
        part = []
        for array in range(3):
            lanes = slice(array * LANES, (array + 1) * LANES)
            real, imag = coarse[:rows, lanes], coarse[rows:, lanes]
            part.append(jnp.concatenate([real * cos + imag * sin, imag * cos - real * sin], axis=1))
        return split(jnp.concatenate(part))

    def wide(value):
        return product(value, (second[0], second[1]))

    def mix(spectra):
        grad = spectra[2 * rows :]
        grad_real, grad_imag = grad[:, :LANES], grad[:, LANES:]
        part = []
        for array in range(2):
            other = spectra[array * rows : (array + 1) * rows]
            real, imag = other[:, :LANES], other[:, LANES:]
            part.append(
                jnp.concatenate([real * grad_real + imag * grad_imag, imag * grad_real - real * grad_imag], axis=1)
            )
        return split(jnp.concatenate(part))

    def turn_back(back):
        spread = []
        for array in range(2):
            value = back[array * rows : (array + 1) * rows]
            real, minus = value[:, :LANES], value[:, LANES:]
            spread.append(jnp.concatenate([real * cos + minus * sin, real * sin - minus * cos]))
        return split(jnp.concatenate(spread, axis=1))

    def narrow(value):
        both = dot(last_rows, value[0])
        return both[:height] + both[height:] + dot(last_rows[:height], value[1])

    turned = [turn_out(coarse[:, 3 * channel * LANES : 3 * (channel + 1) * LANES]) for channel in range(channels)]
    spectra = [wide(value) for value in turned]
    mixed = [mix(value) for value in spectra]
    back = [wide(value) for value in mixed]
    spread = [turn_back(value) for value in back]
    result = jnp.concatenate([narrow(value) for value in spread], axis=1)

    cells = height * channels
    total = sum(block[cells : 2 * cells] * block[2 * cells :] for block in blocks)
    owner = lax.broadcasted_iota(jnp.int32, total.shape, 0) % channels
    for channel in range(channels):
        grad_skip_ref[channel] = jnp.sum(jnp.where(owner == channel, total, 0.0))
        mine = pl.ds(channel, height, stride=channels)
        lanes = 2 * channel * LANES
        kept = skips[channel] * blocks[0][pl.ds(2 * cells + channel, height, stride=channels)]
        grad_signal_ref[mine, :] = result[:, lanes : lanes + LANES] + kept
        grad_filter_ref[mine, :] = result[:, lanes + LANES : lanes + 2 * LANES]


def dense(value):
    channels, cells = value.shape
    return value.reshape(channels, cells // LANES, LANES).transpose(1, 0, 2).reshape(-1, LANES)


def undense(value, channels):
    return value.reshape(-1, channels, LANES).transpose(1, 0, 2).reshape(channels, -1)


def gathered_body(signal, filter_taps, grad_out, skip):
    groups = lax.axis_size("seq")
    channels, cells = signal.shape
    length = cells * groups
    rows = length // LANES
    own = jnp.concatenate([dense(filter_taps), dense(signal), dense(grad_out)])
    chans, cores = lax.axis_size("chan"), lax.axis_size("sub")
    steps = routes(groups, cores)
    arrived = []
    for targets in reversed(steps):
        hops = []
        for part, chan, core in itertools.product(range(lax.axis_size("parts")), range(chans), range(cores)):
            ahead = targets[core if part + chan == 0 else cores + core]
            for device, target in enumerate(ahead):
                hops.append(tuple(((part * groups + seq) * chans + chan) * cores + core for seq in (device, target)))
        arrived.insert(0, lax.ppermute(own, ("parts", "seq", "chan", "sub"), hops))
    tables = [jnp.asarray(table) for table in gathered_tables(length, groups)]
    whole = pl.BlockSpec(memory_space=pltpu.VMEM)
    scalar = pl.BlockSpec(memory_space=pltpu.SMEM)
    params = pltpu.CompilerParams(vmem_limit_bytes=24 * 2**20)
    coarse = pl.pallas_call(
        functools.partial(own_kernel, channels),
        out_shape=jax.ShapeDtypeStruct((2 * rows, 3 * channels * LANES), jnp.float32),
        in_specs=[whole] * 5,
        out_specs=whole,
        compiler_params=params,
        cost_estimate=pl.CostEstimate(flops=2**27, bytes_accessed=2**21, transcendentals=0),
        name="own_part",
    )(own, *tables)
    coarse = pl.pallas_call(
        functools.partial(early_kernel, channels, steps[0]),
        out_shape=jax.ShapeDtypeStruct(coarse.shape, jnp.float32),
        in_specs=[whole] * 3,
        out_specs=whole,
        compiler_params=params,
        cost_estimate=pl.CostEstimate(flops=2**27, bytes_accessed=2**21, transcendentals=0),
        name="early_part",
    )(coarse, arrived[0], tables[0])
    shape = jax.ShapeDtypeStruct(dense(signal).shape, jnp.float32)
    grad_signal, grad_filter, grad_skip = pl.pallas_call(
        functools.partial(gathered_kernel, groups, channels, steps[1:]),
        out_shape=(shape, shape, jax.ShapeDtypeStruct((channels,), jnp.float32)),
        in_specs=[whole] + [whole] * (groups + 5),
        out_specs=(whole, whole, scalar),
        compiler_params=params,
        name="correlate",
    )(skip, coarse, own, *arrived, *tables)
    return (undense(grad_signal, channels), undense(grad_filter, channels), grad_skip)


def frequency_order(groups):
    slots = jnp.arange(2 * groups, dtype=jnp.int32)
    halves = slots // 2
    return jnp.where(slots % 2 == 0, halves, jnp.where(halves == 0, groups, 2 * groups - halves))


def phase_table(left_index, right_index, period):
    product = left_index[:, None] * right_index[None, :] % period
    return 2.0 * math.pi / period * product.astype(jnp.float32)


def transform_tables(cells):
    inner_len = 128
    outer_len = cells // inner_len
    outer_range = jnp.arange(outer_len, dtype=jnp.int32)
    inner_range = jnp.arange(inner_len, dtype=jnp.int32)
    outer_phase = phase_table(outer_range, outer_range, outer_len)
    twist_phase = phase_table(outer_range, inner_range, cells)
    inner_phase = phase_table(inner_range, inner_range, inner_len)
    return (
        jnp.cos(outer_phase),
        jnp.sin(outer_phase),
        jnp.cos(twist_phase),
        jnp.sin(twist_phase),
        jnp.cos(inner_phase),
        jnp.sin(inner_phase),
    )


def complex_apply(real_part, imag_part, cos_table, sin_table, pattern, turning):
    first = jnp.einsum(pattern, real_part, cos_table, precision=highest) - turning * jnp.einsum(
        pattern, imag_part, sin_table, precision=highest
    )
    second = jnp.einsum(pattern, imag_part, cos_table, precision=highest) + turning * jnp.einsum(
        pattern, real_part, sin_table, precision=highest
    )
    return (first, second)


def forward_transform(real_part, imag_part, tables):
    outer_cos, outer_sin, twist_cos, twist_sin, inner_cos, inner_sin = tables
    outer_len = outer_cos.shape[0]
    inner_len = inner_cos.shape[0]
    initial = real_part.shape
    folded = initial[:-1] + (outer_len, inner_len)
    real_part = real_part.reshape(folded)
    imag_part = imag_part.reshape(folded)
    real_part, imag_part = complex_apply(
        real_part, imag_part, outer_cos, outer_sin, "...ab,ac->...cb", -1.0
    )
    real_part, imag_part = (
        real_part * twist_cos + imag_part * twist_sin,
        imag_part * twist_cos - real_part * twist_sin,
    )
    real_part, imag_part = complex_apply(
        real_part, imag_part, inner_cos, inner_sin, "...cb,bd->...cd", -1.0
    )
    return (real_part.reshape(initial), imag_part.reshape(initial))


def inverse_transform(real_part, imag_part, tables):
    outer_cos, outer_sin, twist_cos, twist_sin, inner_cos, inner_sin = tables
    outer_len = outer_cos.shape[0]
    inner_len = inner_cos.shape[0]
    initial = real_part.shape
    folded = initial[:-1] + (outer_len, inner_len)
    real_part = real_part.reshape(folded)
    imag_part = imag_part.reshape(folded)
    real_part, imag_part = complex_apply(
        real_part, imag_part, inner_cos, inner_sin, "...cd,bd->...cb", 1.0
    )
    real_part, imag_part = (
        real_part * twist_cos - imag_part * twist_sin,
        imag_part * twist_cos + real_part * twist_sin,
    )
    real_part, imag_part = complex_apply(
        real_part, imag_part, outer_cos, outer_sin, "...cb,ac->...ab", 1.0
    )
    return (real_part.reshape(initial), imag_part.reshape(initial))


def split_body(signal, filter_taps, grad_out, skip):
    groups = lax.axis_size("seq")
    device = lax.axis_index("seq")
    cells = signal.shape[1]
    width = cells // groups
    doubled = 2 * groups
    period = doubled * cells
    freq_slots = frequency_order(groups)
    tables = transform_tables(cells)
    stacked = jnp.stack([signal, filter_taps, grad_out])[:, :, None, :]
    columns = lax.all_to_all(stacked, "seq", split_axis=3, concat_axis=2, tiled=True)
    group_rows = jnp.arange(groups, dtype=jnp.int32)
    group_phase = phase_table(group_rows, freq_slots, doubled)
    group_cos = jnp.cos(group_phase)
    group_sin = jnp.sin(group_phase)
    real_part = jnp.einsum("acpj,pm->acmj", columns, group_cos, precision=highest)
    imag_part = -jnp.einsum("acpj,pm->acmj", columns, group_sin, precision=highest)
    residues = device * width + jnp.arange(width, dtype=jnp.int32)
    twist_phase = phase_table(freq_slots, residues, period)
    twist_cos = jnp.cos(twist_phase)
    twist_sin = jnp.sin(twist_phase)
    twisted_real = real_part * twist_cos + imag_part * twist_sin
    twisted_imag = imag_part * twist_cos - real_part * twist_sin
    outgoing = jnp.stack([twisted_real, twisted_imag], 1)
    spectra = lax.all_to_all(outgoing, "seq", split_axis=3, concat_axis=4, tiled=True)
    freq_real, freq_imag = forward_transform(spectra[:, 0], spectra[:, 1], tables)
    grad_real = freq_real[-1]
    grad_imag = freq_imag[-1]
    signal_real, signal_imag = (freq_real[0], freq_imag[0])
    filter_real, filter_imag = (freq_real[1], freq_imag[1])
    input_real = filter_real * grad_real + filter_imag * grad_imag
    input_imag = filter_real * grad_imag - filter_imag * grad_real
    taps_real = signal_real * grad_real + signal_imag * grad_imag
    taps_imag = signal_real * grad_imag - signal_imag * grad_real
    back_real = jnp.stack([input_real, taps_real])
    back_imag = jnp.stack([input_imag, taps_imag])
    inverse_real, inverse_imag = inverse_transform(back_real, back_imag, tables)
    full_range = jnp.arange(cells, dtype=jnp.int32)
    local_slots = lax.dynamic_slice_in_dim(freq_slots, 2 * device, 2)
    back_phase = phase_table(local_slots, full_range, period)
    back_cos = jnp.cos(back_phase)
    back_sin = jnp.sin(back_phase)
    turned_real = inverse_real * back_cos - inverse_imag * back_sin
    turned_imag = inverse_imag * back_cos + inverse_real * back_sin
    returning = jnp.stack([turned_real, turned_imag], 1)
    residue_rows = lax.all_to_all(returning, "seq", split_axis=4, concat_axis=3, tiled=True)
    scale = 1.0 / period
    real_out = (
        jnp.einsum("ncmj,pm->ncpj", residue_rows[:, 0], group_cos, precision=highest)
        - jnp.einsum("ncmj,pm->ncpj", residue_rows[:, 1], group_sin, precision=highest)
    ) * scale
    gathered = lax.all_to_all(real_out, "seq", split_axis=2, concat_axis=3, tiled=True)
    grad_signal = gathered[0, :, 0, :] + skip[:, None] * grad_out
    grad_filter = gathered[1, :, 0, :]
    grad_skip = lax.psum(jnp.sum(grad_out * signal, axis=1), "seq")
    return (grad_signal, grad_filter, grad_skip)


def body(signal, filter_taps, grad_out, skip):
    groups = lax.axis_size("seq")
    channels, cells = signal.shape
    whole_fits = channels * cells * groups <= 2**15
    if whole_fits and groups <= 8 and cells % (16 * LANES) == 0:
        return gathered_body(signal, filter_taps, grad_out, skip)
    return split_body(signal, filter_taps, grad_out, skip)
def solution(mesh):
    return jax.shard_map(
        body,
        mesh=mesh,
        in_specs=(
            P(("parts", "chan", "sub"), "seq"),
            P(("parts", "chan", "sub"), "seq"),
            P(("parts", "chan", "sub"), "seq"),
            P(("parts", "chan", "sub")),
        ),
        out_specs=(
            P(("parts", "chan", "sub"), "seq"),
            P(("parts", "chan", "sub"), "seq"),
            P(("parts", "chan", "sub")),
        ),
        check_vma=False,
    )
```

```python
import functools
import math

import jax
import jax.numpy as jnp
import ml_dtypes
import numpy as np
from jax import lax
from jax.experimental import pallas as pl
from jax.experimental.pallas import tpu as pltpu
from jax.sharding import PartitionSpec as P

LANES = 128
highest = lax.Precision.HIGHEST


def split_table(table):
    high = table.astype(np.float32).astype(ml_dtypes.bfloat16)
    low = (table - high.astype(np.float64)).astype(np.float32).astype(ml_dtypes.bfloat16)
    return high, low


def gathered_tables(length, groups):
    rows = length // LANES
    coarse = np.arange(rows, dtype=np.float64)
    fine = np.arange(LANES, dtype=np.float64)
    phase = 2.0 * np.pi / rows * (coarse[:, None] + 0.25) * coarse[None, :]
    first = np.concatenate([np.cos(phase), -np.sin(phase)])
    high, low = (part.reshape(2 * rows, groups, -1) for part in split_table(first))
    stage_first = np.concatenate([high, high, low, low], axis=2).reshape(2 * rows, 4 * rows)
    last = (first.T / length).reshape(groups, rows // groups, 2 * rows)
    turn = 2.0 * np.pi / length * (coarse[:, None] + 0.25) * fine[None, :]
    twiddle = np.stack([np.cos(turn), np.sin(turn)]).astype(np.float32)
    angle = 2.0 * np.pi / LANES * fine[:, None] * fine[None, :]
    cos, sin = np.cos(angle), np.sin(angle)
    second = np.block([[cos, -sin], [sin, cos]])
    return stage_first, twiddle, np.stack(split_table(second)), np.concatenate(split_table(last), axis=1)


def split(value):
    high = value.astype(jnp.bfloat16)
    return high, (value - high.astype(jnp.float32)).astype(jnp.bfloat16)


def dot(left, right):
    return jnp.dot(left, right, preferred_element_type=jnp.float32)


def product(left, right):
    rows = left[0].shape[0]
    both = dot(jnp.concatenate(left), right[0])
    return both[:rows] + both[rows:] + dot(left[0], right[1])


def stage_rows(block, channels):
    cells = block.shape[0] // 3
    pieces = []
    for channel in range(channels):
        for array in range(3):
            pieces.append(block[pl.ds(array * cells + channel, cells // channels, stride=channels)])
    value = jnp.concatenate(pieces, axis=1)
    high, low = split(value)
    return jnp.concatenate([high, low, high, low])


def stage_columns(table, group):
    width = table.shape[1] // lax.axis_size("seq")
    return table[:, pl.ds(pl.multiple_of(group * width, width), width)]


def routes(groups, cores):
    plans = [(tuple(range(groups)), tuple(range(1, groups)))]
    if groups == 4:
        plans = [((0, 2, 1, 3), (3, 1, 2)), ((0, 1, 3, 2), (1, 2, 3))]
    steps = []
    for index in range(groups - 1):
        targets = []
        for core in range(cores):
            cycle, moves = plans[core % len(plans)]
            ahead = {cycle[place]: cycle[(place + moves[index]) % groups] for place in range(groups)}
            targets.append([ahead[device] for device in range(groups)])
        steps.append(targets)
    return steps


def sender(targets):
    code = 0
    for core, ahead in enumerate(targets):
        packed = sum(device << 4 * target for device, target in enumerate(ahead))
        code = jnp.where(lax.axis_index("sub") == core, packed, code)
    return lax.bitwise_and(lax.shift_right_logical(code, 4 * lax.axis_index("seq")), 15)


def own_kernel(channels, block, first, twiddle, second, last, out_ref):
    out_ref[...] = dot(stage_columns(first, lax.axis_index("seq")), stage_rows(block, channels))


def early_kernel(channels, targets, coarse_ref, block, first, out_ref):
    out_ref[...] = coarse_ref[...] + dot(stage_columns(first, sender(targets)), stage_rows(block, channels))


def gathered_kernel(groups, channels, late, skip_ref, coarse_ref, *refs):
    blocks = refs[:groups]
    first, twiddle, second, last = refs[groups : groups + 4]
    grad_signal_ref, grad_filter_ref, grad_skip_ref = refs[groups + 4 :]
    skips = skip_ref[...]
    device = lax.axis_index("seq")
    rows = twiddle.shape[1]
    height = rows // groups

    columns = jnp.concatenate([stage_columns(first, sender(targets)) for targets in late], axis=1)
    data = jnp.concatenate([stage_rows(block, channels) for block in blocks[groups - len(late) :]])
    cos, sin = twiddle[0], twiddle[1]
    last_rows = last[device]

    coarse = coarse_ref[...] + dot(columns, data)

    def turn_out(coarse):
        part = []
        for array in range(3):
            lanes = slice(array * LANES, (array + 1) * LANES)
            real, imag = coarse[:rows, lanes], coarse[rows:, lanes]
            part.append(jnp.concatenate([real * cos + imag * sin, imag * cos - real * sin], axis=1))
        return split(jnp.concatenate(part))

    def wide(value):
        return product(value, (second[0], second[1]))

    def mix(spectra):
        grad = spectra[2 * rows :]
        grad_real, grad_imag = grad[:, :LANES], grad[:, LANES:]
        part = []
        for array in range(2):
            other = spectra[array * rows : (array + 1) * rows]
            real, imag = other[:, :LANES], other[:, LANES:]
            part.append(
                jnp.concatenate([real * grad_real + imag * grad_imag, imag * grad_real - real * grad_imag], axis=1)
            )
        return split(jnp.concatenate(part))

    def turn_back(back):
        spread = []
        for array in range(2):
            value = back[array * rows : (array + 1) * rows]
            real, minus = value[:, :LANES], value[:, LANES:]
            spread.append(jnp.concatenate([real * cos + minus * sin, real * sin - minus * cos]))
        return split(jnp.concatenate(spread, axis=1))

    def narrow(value):
        both = dot(last_rows, value[0])
        return both[:height] + both[height:] + dot(last_rows[:height], value[1])

    turned = [turn_out(coarse[:, 3 * channel * LANES : 3 * (channel + 1) * LANES]) for channel in range(channels)]
    spectra = [wide(value) for value in turned]
    mixed = [mix(value) for value in spectra]
    back = [wide(value) for value in mixed]
    spread = [turn_back(value) for value in back]
    result = jnp.concatenate([narrow(value) for value in spread], axis=1)

    cells = height * channels
    total = sum(block[cells : 2 * cells] * block[2 * cells :] for block in blocks)
    owner = lax.broadcasted_iota(jnp.int32, total.shape, 0) % channels
    for channel in range(channels):
        grad_skip_ref[channel] = jnp.sum(jnp.where(owner == channel, total, 0.0))
        mine = pl.ds(channel, height, stride=channels)
        lanes = 2 * channel * LANES
        kept = skips[channel] * blocks[0][pl.ds(2 * cells + channel, height, stride=channels)]
        grad_signal_ref[mine, :] = result[:, lanes : lanes + LANES] + kept
        grad_filter_ref[mine, :] = result[:, lanes + LANES : lanes + 2 * LANES]


def dense(value):
    channels, cells = value.shape
    return value.reshape(channels, cells // LANES, LANES).transpose(1, 0, 2).reshape(-1, LANES)


def undense(value, channels):
    return value.reshape(-1, channels, LANES).transpose(1, 0, 2).reshape(channels, -1)


def gathered_body(signal, filter_taps, grad_out, skip):
    groups = lax.axis_size("seq")
    channels, cells = signal.shape
    length = cells * groups
    rows = length // LANES
    own = jnp.concatenate([dense(filter_taps), dense(signal), dense(grad_out)])
    cores = lax.axis_size("sub")
    steps = routes(groups, cores)
    arrived = []
    for targets in reversed(steps):
        hops = []
        for core, ahead in enumerate(targets):
            hops += [(device * cores + core, target * cores + core) for device, target in enumerate(ahead)]
        arrived.insert(0, lax.ppermute(own, ("seq", "sub"), hops))
    tables = [jnp.asarray(table) for table in gathered_tables(length, groups)]
    whole = pl.BlockSpec(memory_space=pltpu.VMEM)
    scalar = pl.BlockSpec(memory_space=pltpu.SMEM)
    params = pltpu.CompilerParams(vmem_limit_bytes=24 * 2**20)
    coarse = pl.pallas_call(
        functools.partial(own_kernel, channels),
        out_shape=jax.ShapeDtypeStruct((2 * rows, 3 * channels * LANES), jnp.float32),
        in_specs=[whole] * 5,
        out_specs=whole,
        compiler_params=params,
        cost_estimate=pl.CostEstimate(flops=2**27, bytes_accessed=2**21, transcendentals=0),
        name="own_part",
    )(own, *tables)
    coarse = pl.pallas_call(
        functools.partial(early_kernel, channels, steps[0]),
        out_shape=jax.ShapeDtypeStruct(coarse.shape, jnp.float32),
        in_specs=[whole] * 3,
        out_specs=whole,
        compiler_params=params,
        cost_estimate=pl.CostEstimate(flops=2**27, bytes_accessed=2**21, transcendentals=0),
        name="early_part",
    )(coarse, arrived[0], tables[0])
    shape = jax.ShapeDtypeStruct(dense(signal).shape, jnp.float32)
    grad_signal, grad_filter, grad_skip = pl.pallas_call(
        functools.partial(gathered_kernel, groups, channels, steps[1:]),
        out_shape=(shape, shape, jax.ShapeDtypeStruct((channels,), jnp.float32)),
        in_specs=[whole] + [whole] * (groups + 5),
        out_specs=(whole, whole, scalar),
        compiler_params=params,
        name="correlate",
    )(skip, coarse, own, *arrived, *tables)
    return (undense(grad_signal, channels), undense(grad_filter, channels), grad_skip)


def frequency_order(groups):
    slots = jnp.arange(2 * groups, dtype=jnp.int32)
    halves = slots // 2
    return jnp.where(slots % 2 == 0, halves, jnp.where(halves == 0, groups, 2 * groups - halves))


def phase_table(left_index, right_index, period):
    product = left_index[:, None] * right_index[None, :] % period
    return 2.0 * math.pi / period * product.astype(jnp.float32)


def transform_tables(cells):
    inner_len = 128
    outer_len = cells // inner_len
    outer_range = jnp.arange(outer_len, dtype=jnp.int32)
    inner_range = jnp.arange(inner_len, dtype=jnp.int32)
    outer_phase = phase_table(outer_range, outer_range, outer_len)
    twist_phase = phase_table(outer_range, inner_range, cells)
    inner_phase = phase_table(inner_range, inner_range, inner_len)
    return (
        jnp.cos(outer_phase),
        jnp.sin(outer_phase),
        jnp.cos(twist_phase),
        jnp.sin(twist_phase),
        jnp.cos(inner_phase),
        jnp.sin(inner_phase),
    )


def complex_apply(real_part, imag_part, cos_table, sin_table, pattern, turning):
    first = jnp.einsum(pattern, real_part, cos_table, precision=highest) - turning * jnp.einsum(
        pattern, imag_part, sin_table, precision=highest
    )
    second = jnp.einsum(pattern, imag_part, cos_table, precision=highest) + turning * jnp.einsum(
        pattern, real_part, sin_table, precision=highest
    )
    return (first, second)


def forward_transform(real_part, imag_part, tables):
    outer_cos, outer_sin, twist_cos, twist_sin, inner_cos, inner_sin = tables
    outer_len = outer_cos.shape[0]
    inner_len = inner_cos.shape[0]
    initial = real_part.shape
    folded = initial[:-1] + (outer_len, inner_len)
    real_part = real_part.reshape(folded)
    imag_part = imag_part.reshape(folded)
    real_part, imag_part = complex_apply(
        real_part, imag_part, outer_cos, outer_sin, "...ab,ac->...cb", -1.0
    )
    real_part, imag_part = (
        real_part * twist_cos + imag_part * twist_sin,
        imag_part * twist_cos - real_part * twist_sin,
    )
    real_part, imag_part = complex_apply(
        real_part, imag_part, inner_cos, inner_sin, "...cb,bd->...cd", -1.0
    )
    return (real_part.reshape(initial), imag_part.reshape(initial))


def inverse_transform(real_part, imag_part, tables):
    outer_cos, outer_sin, twist_cos, twist_sin, inner_cos, inner_sin = tables
    outer_len = outer_cos.shape[0]
    inner_len = inner_cos.shape[0]
    initial = real_part.shape
    folded = initial[:-1] + (outer_len, inner_len)
    real_part = real_part.reshape(folded)
    imag_part = imag_part.reshape(folded)
    real_part, imag_part = complex_apply(
        real_part, imag_part, inner_cos, inner_sin, "...cd,bd->...cb", 1.0
    )
    real_part, imag_part = (
        real_part * twist_cos - imag_part * twist_sin,
        imag_part * twist_cos + real_part * twist_sin,
    )
    real_part, imag_part = complex_apply(
        real_part, imag_part, outer_cos, outer_sin, "...cb,ac->...ab", 1.0
    )
    return (real_part.reshape(initial), imag_part.reshape(initial))


def split_body(signal, filter_taps, grad_out, skip):
    groups = lax.axis_size("seq")
    device = lax.axis_index("seq")
    cells = signal.shape[1]
    width = cells // groups
    doubled = 2 * groups
    period = doubled * cells
    freq_slots = frequency_order(groups)
    tables = transform_tables(cells)
    stacked = jnp.stack([signal, filter_taps, grad_out])[:, :, None, :]
    columns = lax.all_to_all(stacked, "seq", split_axis=3, concat_axis=2, tiled=True)
    group_rows = jnp.arange(groups, dtype=jnp.int32)
    group_phase = phase_table(group_rows, freq_slots, doubled)
    group_cos = jnp.cos(group_phase)
    group_sin = jnp.sin(group_phase)
    real_part = jnp.einsum("acpj,pm->acmj", columns, group_cos, precision=highest)
    imag_part = -jnp.einsum("acpj,pm->acmj", columns, group_sin, precision=highest)
    residues = device * width + jnp.arange(width, dtype=jnp.int32)
    twist_phase = phase_table(freq_slots, residues, period)
    twist_cos = jnp.cos(twist_phase)
    twist_sin = jnp.sin(twist_phase)
    twisted_real = real_part * twist_cos + imag_part * twist_sin
    twisted_imag = imag_part * twist_cos - real_part * twist_sin
    outgoing = jnp.stack([twisted_real, twisted_imag], 1)
    spectra = lax.all_to_all(outgoing, "seq", split_axis=3, concat_axis=4, tiled=True)
    freq_real, freq_imag = forward_transform(spectra[:, 0], spectra[:, 1], tables)
    grad_real = freq_real[-1]
    grad_imag = freq_imag[-1]
    signal_real, signal_imag = (freq_real[0], freq_imag[0])
    filter_real, filter_imag = (freq_real[1], freq_imag[1])
    input_real = filter_real * grad_real + filter_imag * grad_imag
    input_imag = filter_real * grad_imag - filter_imag * grad_real
    taps_real = signal_real * grad_real + signal_imag * grad_imag
    taps_imag = signal_real * grad_imag - signal_imag * grad_real
    back_real = jnp.stack([input_real, taps_real])
    back_imag = jnp.stack([input_imag, taps_imag])
    inverse_real, inverse_imag = inverse_transform(back_real, back_imag, tables)
    full_range = jnp.arange(cells, dtype=jnp.int32)
    local_slots = lax.dynamic_slice_in_dim(freq_slots, 2 * device, 2)
    back_phase = phase_table(local_slots, full_range, period)
    back_cos = jnp.cos(back_phase)
    back_sin = jnp.sin(back_phase)
    turned_real = inverse_real * back_cos - inverse_imag * back_sin
    turned_imag = inverse_imag * back_cos + inverse_real * back_sin
    returning = jnp.stack([turned_real, turned_imag], 1)
    residue_rows = lax.all_to_all(returning, "seq", split_axis=4, concat_axis=3, tiled=True)
    scale = 1.0 / period
    real_out = (
        jnp.einsum("ncmj,pm->ncpj", residue_rows[:, 0], group_cos, precision=highest)
        - jnp.einsum("ncmj,pm->ncpj", residue_rows[:, 1], group_sin, precision=highest)
    ) * scale
    gathered = lax.all_to_all(real_out, "seq", split_axis=2, concat_axis=3, tiled=True)
    grad_signal = gathered[0, :, 0, :] + skip[:, None] * grad_out
    grad_filter = gathered[1, :, 0, :]
    grad_skip = lax.psum(jnp.sum(grad_out * signal, axis=1), "seq")
    return (grad_signal, grad_filter, grad_skip)


def body(signal, filter_taps, grad_out, skip):
    groups = lax.axis_size("seq")
    channels, cells = signal.shape
    whole_fits = channels * cells * groups <= 2**15
    if whole_fits and groups <= 8 and cells % (16 * LANES) == 0:
        return gathered_body(signal, filter_taps, grad_out, skip)
    return split_body(signal, filter_taps, grad_out, skip)
def solution(mesh):
    return jax.shard_map(
        body,
        mesh=mesh,
        in_specs=(
            P(("parts", "chan", "sub"), "seq"),
            P(("parts", "chan", "sub"), "seq"),
            P(("parts", "chan", "sub"), "seq"),
            P(("parts", "chan", "sub")),
        ),
        out_specs=(
            P(("parts", "chan", "sub"), "seq"),
            P(("parts", "chan", "sub"), "seq"),
            P(("parts", "chan", "sub")),
        ),
        check_vma=False,
    )
```

```python
import functools
import math

import jax
import jax.numpy as jnp
import ml_dtypes
import numpy as np
from jax import lax
from jax.experimental import pallas as pl
from jax.experimental.pallas import tpu as pltpu
from jax.sharding import PartitionSpec as P

LANES = 128
highest = lax.Precision.HIGHEST


def split_table(table):
    high = table.astype(np.float32).astype(ml_dtypes.bfloat16)
    low = (table - high.astype(np.float64)).astype(np.float32).astype(ml_dtypes.bfloat16)
    return high, low


def gathered_tables(length, groups):
    rows = length // LANES
    coarse = np.arange(rows, dtype=np.float64)
    fine = np.arange(LANES, dtype=np.float64)
    phase = 2.0 * np.pi / rows * (coarse[:, None] + 0.25) * coarse[None, :]
    first = np.concatenate([np.cos(phase), -np.sin(phase)])
    high, low = (part.reshape(2 * rows, groups, -1) for part in split_table(first))
    stage_first = np.concatenate([high, high, low, low], axis=2).reshape(2 * rows, 4 * rows)
    last = (first.T / length).reshape(groups, rows // groups, 2 * rows)
    turn = 2.0 * np.pi / length * (coarse[:, None] + 0.25) * fine[None, :]
    twiddle = np.stack([np.cos(turn), np.sin(turn)]).astype(np.float32)
    angle = 2.0 * np.pi / LANES * fine[:, None] * fine[None, :]
    cos, sin = np.cos(angle), np.sin(angle)
    second = np.block([[cos, -sin], [sin, cos]])
    return stage_first, twiddle, np.stack(split_table(second)), np.concatenate(split_table(last), axis=1)


def split(value):
    high = value.astype(jnp.bfloat16)
    return high, (value - high.astype(jnp.float32)).astype(jnp.bfloat16)


def dot(left, right):
    return jnp.dot(left, right, preferred_element_type=jnp.float32)


def product(left, right):
    return dot(jnp.concatenate([left[0], left[0], left[1]], axis=1), jnp.concatenate([right[0], right[1], right[0]]))


def stage_rows(block, channels):
    cells = block.shape[0] // 3
    pieces = []
    for channel in range(channels):
        for array in range(3):
            pieces.append(block[pl.ds(array * cells + channel, cells // channels, stride=channels)])
    value = jnp.concatenate(pieces, axis=1)
    high, low = split(value)
    return jnp.concatenate([high, low, high, low])


def stage_columns(table, group):
    width = table.shape[1] // lax.axis_size("seq")
    return table[:, pl.ds(pl.multiple_of(group * width, width), width)]


def routes(groups, cores):
    plans = [(tuple(range(groups)), tuple(range(1, groups)))]
    if groups == 4:
        plans = [((0, 2, 1, 3), (3, 1, 2)), ((0, 1, 3, 2), (1, 2, 3))]
    steps = []
    for index in range(groups - 1):
        targets = []
        for core in range(cores):
            cycle, moves = plans[core % len(plans)]
            ahead = {cycle[place]: cycle[(place + moves[index]) % groups] for place in range(groups)}
            targets.append([ahead[device] for device in range(groups)])
        steps.append(targets)
    return steps


def sender(targets):
    code = 0
    for core, ahead in enumerate(targets):
        packed = sum(device << 4 * target for device, target in enumerate(ahead))
        code = jnp.where(lax.axis_index("sub") == core, packed, code)
    return lax.bitwise_and(lax.shift_right_logical(code, 4 * lax.axis_index("seq")), 15)


def own_kernel(channels, block, first, twiddle, second, last, out_ref):
    out_ref[...] = dot(stage_columns(first, lax.axis_index("seq")), stage_rows(block, channels))


def gathered_kernel(groups, channels, late, skip_ref, coarse_ref, *refs):
    blocks = refs[:groups]
    first, twiddle, second, last = refs[groups : groups + 4]
    grad_signal_ref, grad_filter_ref, grad_skip_ref = refs[groups + 4 :]
    skips = skip_ref[...]
    device = lax.axis_index("seq")
    rows = twiddle.shape[1]
    height = rows // groups

    columns = jnp.concatenate([stage_columns(first, sender(targets)) for targets in late], axis=1)
    data = jnp.concatenate([stage_rows(block, channels) for block in blocks[groups - len(late) :]])
    cos, sin = twiddle[0], twiddle[1]
    last_rows = last[device]

    coarse = coarse_ref[...] + dot(columns, data)

    def turn_out(coarse):
        part = []
        for array in range(3):
            lanes = slice(array * LANES, (array + 1) * LANES)
            real, imag = coarse[:rows, lanes], coarse[rows:, lanes]
            part.append(jnp.concatenate([real * cos + imag * sin, imag * cos - real * sin], axis=1))
        return split(jnp.concatenate(part))

    def wide(value):
        return product(value, (second[0], second[1]))

    def mix(spectra):
        grad = spectra[2 * rows :]
        grad_real, grad_imag = grad[:, :LANES], grad[:, LANES:]
        part = []
        for array in range(2):
            other = spectra[array * rows : (array + 1) * rows]
            real, imag = other[:, :LANES], other[:, LANES:]
            part.append(
                jnp.concatenate([real * grad_real + imag * grad_imag, imag * grad_real - real * grad_imag], axis=1)
            )
        return split(jnp.concatenate(part))

    def turn_back(back):
        spread = []
        for array in range(2):
            value = back[array * rows : (array + 1) * rows]
            real, minus = value[:, :LANES], value[:, LANES:]
            spread.append(jnp.concatenate([real * cos + minus * sin, real * sin - minus * cos]))
        return split(jnp.concatenate(spread, axis=1))

    def narrow(value):
        both = dot(last_rows, value[0])
        return both[:height] + both[height:] + dot(last_rows[:height], value[1])

    turned = [turn_out(coarse[:, 3 * channel * LANES : 3 * (channel + 1) * LANES]) for channel in range(channels)]
    spectra = [wide(value) for value in turned]
    mixed = [mix(value) for value in spectra]
    back = [wide(value) for value in mixed]
    spread = [turn_back(value) for value in back]
    result = jnp.concatenate([narrow(value) for value in spread], axis=1)

    cells = height * channels
    total = sum(block[cells : 2 * cells] * block[2 * cells :] for block in blocks)
    owner = lax.broadcasted_iota(jnp.int32, total.shape, 0) % channels
    for channel in range(channels):
        grad_skip_ref[channel] = jnp.sum(jnp.where(owner == channel, total, 0.0))
        mine = pl.ds(channel, height, stride=channels)
        lanes = 2 * channel * LANES
        kept = skips[channel] * blocks[0][pl.ds(2 * cells + channel, height, stride=channels)]
        grad_signal_ref[mine, :] = result[:, lanes : lanes + LANES] + kept
        grad_filter_ref[mine, :] = result[:, lanes + LANES : lanes + 2 * LANES]


def dense(value):
    channels, cells = value.shape
    return value.reshape(channels, cells // LANES, LANES).transpose(1, 0, 2).reshape(-1, LANES)


def undense(value, channels):
    return value.reshape(-1, channels, LANES).transpose(1, 0, 2).reshape(channels, -1)


def gathered_body(signal, filter_taps, grad_out, skip):
    groups = lax.axis_size("seq")
    channels, cells = signal.shape
    length = cells * groups
    rows = length // LANES
    own = jnp.concatenate([dense(filter_taps), dense(signal), dense(grad_out)])
    cores = lax.axis_size("sub")
    steps = routes(groups, cores)
    arrived = []
    for targets in reversed(steps):
        hops = []
        for core, ahead in enumerate(targets):
            hops += [(device * cores + core, target * cores + core) for device, target in enumerate(ahead)]
        arrived.insert(0, lax.ppermute(own, ("seq", "sub"), hops))
    tables = [jnp.asarray(table) for table in gathered_tables(length, groups)]
    whole = pl.BlockSpec(memory_space=pltpu.VMEM)
    scalar = pl.BlockSpec(memory_space=pltpu.SMEM)
    params = pltpu.CompilerParams(vmem_limit_bytes=24 * 2**20)
    coarse = pl.pallas_call(
        functools.partial(own_kernel, channels),
        out_shape=jax.ShapeDtypeStruct((2 * rows, 3 * channels * LANES), jnp.float32),
        in_specs=[whole] * 5,
        out_specs=whole,
        compiler_params=params,
        cost_estimate=pl.CostEstimate(flops=2**27, bytes_accessed=2**21, transcendentals=0),
        name="own_part",
    )(own, *tables)
    shape = jax.ShapeDtypeStruct(dense(signal).shape, jnp.float32)
    grad_signal, grad_filter, grad_skip = pl.pallas_call(
        functools.partial(gathered_kernel, groups, channels, steps[::-1]),
        out_shape=(shape, shape, jax.ShapeDtypeStruct((channels,), jnp.float32)),
        in_specs=[whole] + [whole] * (groups + 5),
        out_specs=(whole, whole, scalar),
        compiler_params=params,
        name="correlate",
    )(skip, coarse, own, *arrived[::-1], *tables)
    return (undense(grad_signal, channels), undense(grad_filter, channels), grad_skip)


def frequency_order(groups):
    slots = jnp.arange(2 * groups, dtype=jnp.int32)
    halves = slots // 2
    return jnp.where(slots % 2 == 0, halves, jnp.where(halves == 0, groups, 2 * groups - halves))


def phase_table(left_index, right_index, period):
    product = left_index[:, None] * right_index[None, :] % period
    return 2.0 * math.pi / period * product.astype(jnp.float32)


def transform_tables(cells):
    inner_len = 128
    outer_len = cells // inner_len
    outer_range = jnp.arange(outer_len, dtype=jnp.int32)
    inner_range = jnp.arange(inner_len, dtype=jnp.int32)
    outer_phase = phase_table(outer_range, outer_range, outer_len)
    twist_phase = phase_table(outer_range, inner_range, cells)
    inner_phase = phase_table(inner_range, inner_range, inner_len)
    return (
        jnp.cos(outer_phase),
        jnp.sin(outer_phase),
        jnp.cos(twist_phase),
        jnp.sin(twist_phase),
        jnp.cos(inner_phase),
        jnp.sin(inner_phase),
    )


def complex_apply(real_part, imag_part, cos_table, sin_table, pattern, turning):
    first = jnp.einsum(pattern, real_part, cos_table, precision=highest) - turning * jnp.einsum(
        pattern, imag_part, sin_table, precision=highest
    )
    second = jnp.einsum(pattern, imag_part, cos_table, precision=highest) + turning * jnp.einsum(
        pattern, real_part, sin_table, precision=highest
    )
    return (first, second)


def forward_transform(real_part, imag_part, tables):
    outer_cos, outer_sin, twist_cos, twist_sin, inner_cos, inner_sin = tables
    outer_len = outer_cos.shape[0]
    inner_len = inner_cos.shape[0]
    initial = real_part.shape
    folded = initial[:-1] + (outer_len, inner_len)
    real_part = real_part.reshape(folded)
    imag_part = imag_part.reshape(folded)
    real_part, imag_part = complex_apply(
        real_part, imag_part, outer_cos, outer_sin, "...ab,ac->...cb", -1.0
    )
    real_part, imag_part = (
        real_part * twist_cos + imag_part * twist_sin,
        imag_part * twist_cos - real_part * twist_sin,
    )
    real_part, imag_part = complex_apply(
        real_part, imag_part, inner_cos, inner_sin, "...cb,bd->...cd", -1.0
    )
    return (real_part.reshape(initial), imag_part.reshape(initial))


def inverse_transform(real_part, imag_part, tables):
    outer_cos, outer_sin, twist_cos, twist_sin, inner_cos, inner_sin = tables
    outer_len = outer_cos.shape[0]
    inner_len = inner_cos.shape[0]
    initial = real_part.shape
    folded = initial[:-1] + (outer_len, inner_len)
    real_part = real_part.reshape(folded)
    imag_part = imag_part.reshape(folded)
    real_part, imag_part = complex_apply(
        real_part, imag_part, inner_cos, inner_sin, "...cd,bd->...cb", 1.0
    )
    real_part, imag_part = (
        real_part * twist_cos - imag_part * twist_sin,
        imag_part * twist_cos + real_part * twist_sin,
    )
    real_part, imag_part = complex_apply(
        real_part, imag_part, outer_cos, outer_sin, "...cb,ac->...ab", 1.0
    )
    return (real_part.reshape(initial), imag_part.reshape(initial))


def split_body(signal, filter_taps, grad_out, skip):
    groups = lax.axis_size("seq")
    device = lax.axis_index("seq")
    cells = signal.shape[1]
    width = cells // groups
    doubled = 2 * groups
    period = doubled * cells
    freq_slots = frequency_order(groups)
    tables = transform_tables(cells)
    stacked = jnp.stack([signal, filter_taps, grad_out])[:, :, None, :]
    columns = lax.all_to_all(stacked, "seq", split_axis=3, concat_axis=2, tiled=True)
    group_rows = jnp.arange(groups, dtype=jnp.int32)
    group_phase = phase_table(group_rows, freq_slots, doubled)
    group_cos = jnp.cos(group_phase)
    group_sin = jnp.sin(group_phase)
    real_part = jnp.einsum("acpj,pm->acmj", columns, group_cos, precision=highest)
    imag_part = -jnp.einsum("acpj,pm->acmj", columns, group_sin, precision=highest)
    residues = device * width + jnp.arange(width, dtype=jnp.int32)
    twist_phase = phase_table(freq_slots, residues, period)
    twist_cos = jnp.cos(twist_phase)
    twist_sin = jnp.sin(twist_phase)
    twisted_real = real_part * twist_cos + imag_part * twist_sin
    twisted_imag = imag_part * twist_cos - real_part * twist_sin
    outgoing = jnp.stack([twisted_real, twisted_imag], 1)
    spectra = lax.all_to_all(outgoing, "seq", split_axis=3, concat_axis=4, tiled=True)
    freq_real, freq_imag = forward_transform(spectra[:, 0], spectra[:, 1], tables)
    grad_real = freq_real[-1]
    grad_imag = freq_imag[-1]
    signal_real, signal_imag = (freq_real[0], freq_imag[0])
    filter_real, filter_imag = (freq_real[1], freq_imag[1])
    input_real = filter_real * grad_real + filter_imag * grad_imag
    input_imag = filter_real * grad_imag - filter_imag * grad_real
    taps_real = signal_real * grad_real + signal_imag * grad_imag
    taps_imag = signal_real * grad_imag - signal_imag * grad_real
    back_real = jnp.stack([input_real, taps_real])
    back_imag = jnp.stack([input_imag, taps_imag])
    inverse_real, inverse_imag = inverse_transform(back_real, back_imag, tables)
    full_range = jnp.arange(cells, dtype=jnp.int32)
    local_slots = lax.dynamic_slice_in_dim(freq_slots, 2 * device, 2)
    back_phase = phase_table(local_slots, full_range, period)
    back_cos = jnp.cos(back_phase)
    back_sin = jnp.sin(back_phase)
    turned_real = inverse_real * back_cos - inverse_imag * back_sin
    turned_imag = inverse_imag * back_cos + inverse_real * back_sin
    returning = jnp.stack([turned_real, turned_imag], 1)
    residue_rows = lax.all_to_all(returning, "seq", split_axis=4, concat_axis=3, tiled=True)
    scale = 1.0 / period
    real_out = (
        jnp.einsum("ncmj,pm->ncpj", residue_rows[:, 0], group_cos, precision=highest)
        - jnp.einsum("ncmj,pm->ncpj", residue_rows[:, 1], group_sin, precision=highest)
    ) * scale
    gathered = lax.all_to_all(real_out, "seq", split_axis=2, concat_axis=3, tiled=True)
    grad_signal = gathered[0, :, 0, :] + skip[:, None] * grad_out
    grad_filter = gathered[1, :, 0, :]
    grad_skip = lax.psum(jnp.sum(grad_out * signal, axis=1), "seq")
    return (grad_signal, grad_filter, grad_skip)


def body(signal, filter_taps, grad_out, skip):
    groups = lax.axis_size("seq")
    channels, cells = signal.shape
    whole_fits = channels * cells * groups <= 2**15
    if whole_fits and groups <= 8 and cells % (16 * LANES) == 0:
        return gathered_body(signal, filter_taps, grad_out, skip)
    return split_body(signal, filter_taps, grad_out, skip)
def solution(mesh):
    return jax.shard_map(
        body,
        mesh=mesh,
        in_specs=(
            P(("parts", "chan", "sub"), "seq"),
            P(("parts", "chan", "sub"), "seq"),
            P(("parts", "chan", "sub"), "seq"),
            P(("parts", "chan", "sub")),
        ),
        out_specs=(
            P(("parts", "chan", "sub"), "seq"),
            P(("parts", "chan", "sub"), "seq"),
            P(("parts", "chan", "sub")),
        ),
        check_vma=False,
    )
```

```python
import functools
import math

import jax
import jax.numpy as jnp
import ml_dtypes
import numpy as np
from jax import lax
from jax.experimental import pallas as pl
from jax.experimental.pallas import tpu as pltpu
from jax.sharding import PartitionSpec as P

LANES = 128
highest = lax.Precision.HIGHEST


def split_table(table):
    high = table.astype(np.float32).astype(ml_dtypes.bfloat16)
    low = (table - high.astype(np.float64)).astype(np.float32).astype(ml_dtypes.bfloat16)
    return high, low


def gathered_tables(length, groups):
    rows = length // LANES
    coarse = np.arange(rows, dtype=np.float64)
    fine = np.arange(LANES, dtype=np.float64)
    phase = 2.0 * np.pi / rows * (coarse[:, None] + 0.25) * coarse[None, :]
    first = np.concatenate([np.cos(phase), -np.sin(phase)])
    high, low = (part.reshape(2 * rows, groups, -1) for part in split_table(first))
    stage_first = np.concatenate([high, high, low, low], axis=2).reshape(2 * rows, 4 * rows)
    last = (first.T / length).reshape(groups, rows // groups, 2 * rows)
    turn = 2.0 * np.pi / length * (coarse[:, None] + 0.25) * fine[None, :]
    twiddle = np.stack([np.cos(turn), np.sin(turn)]).astype(np.float32)
    angle = 2.0 * np.pi / LANES * fine[:, None] * fine[None, :]
    cos, sin = np.cos(angle), np.sin(angle)
    second = np.block([[cos, -sin], [sin, cos]])
    return stage_first, twiddle, np.stack(split_table(second)), np.concatenate(split_table(last), axis=1)


def split(value):
    high = value.astype(jnp.bfloat16)
    return high, (value - high.astype(jnp.float32)).astype(jnp.bfloat16)


def dot(left, right):
    return jnp.dot(left, right, preferred_element_type=jnp.float32)


def product(left, right):
    return dot(jnp.concatenate([left[0], left[0], left[1]], axis=1), jnp.concatenate([right[0], right[1], right[0]]))


def stage_rows(block, channels):
    cells = block.shape[0] // 3
    pieces = []
    for channel in range(channels):
        for array in range(3):
            pieces.append(block[pl.ds(array * cells + channel, cells // channels, stride=channels)])
    value = jnp.concatenate(pieces, axis=1)
    high, low = split(value)
    return jnp.concatenate([high, low, high, low])


def stage_columns(table, group):
    width = table.shape[1] // lax.axis_size("seq")
    return table[:, pl.ds(pl.multiple_of(group * width, width), width)]


def routes(groups, cores):
    plans = [(tuple(range(groups)), tuple(range(1, groups)))]
    if groups == 4:
        plans = [((0, 2, 1, 3), (3, 1, 2)), ((0, 1, 3, 2), (1, 2, 3))]
    steps = []
    for index in range(groups - 1):
        targets = []
        for core in range(cores):
            cycle, moves = plans[core % len(plans)]
            ahead = {cycle[place]: cycle[(place + moves[index]) % groups] for place in range(groups)}
            targets.append([ahead[device] for device in range(groups)])
        steps.append(targets)
    return steps


def sender(targets):
    code = 0
    for core, ahead in enumerate(targets):
        packed = sum(device << 4 * target for device, target in enumerate(ahead))
        code = jnp.where(lax.axis_index("sub") == core, packed, code)
    return lax.bitwise_and(lax.shift_right_logical(code, 4 * lax.axis_index("seq")), 15)


def own_kernel(channels, block, first, twiddle, second, last, out_ref):
    out_ref[...] = dot(stage_columns(first, lax.axis_index("seq")), stage_rows(block, channels))


def early_kernel(channels, targets, coarse_ref, block, first, out_ref):
    out_ref[...] = coarse_ref[...] + dot(stage_columns(first, sender(targets)), stage_rows(block, channels))


def gathered_kernel(groups, channels, late, skip_ref, coarse_ref, *refs):
    blocks = refs[:groups]
    first, twiddle, second, last = refs[groups : groups + 4]
    grad_signal_ref, grad_filter_ref, grad_skip_ref = refs[groups + 4 :]
    skips = skip_ref[...]
    device = lax.axis_index("seq")
    rows = twiddle.shape[1]
    height = rows // groups

    columns = jnp.concatenate([stage_columns(first, sender(targets)) for targets in late], axis=1)
    data = jnp.concatenate([stage_rows(block, channels) for block in blocks[groups - len(late) :]])
    cos, sin = twiddle[0], twiddle[1]
    last_rows = last[device]

    coarse = coarse_ref[...] + dot(columns, data)

    def turn_out(coarse):
        part = []
        for array in range(3):
            lanes = slice(array * LANES, (array + 1) * LANES)
            real, imag = coarse[:rows, lanes], coarse[rows:, lanes]
            part.append(jnp.concatenate([real * cos + imag * sin, imag * cos - real * sin], axis=1))
        return split(jnp.concatenate(part))

    def wide(value):
        return product(value, (second[0], second[1]))

    def mix(spectra):
        grad = spectra[2 * rows :]
        grad_real, grad_imag = grad[:, :LANES], grad[:, LANES:]
        part = []
        for array in range(2):
            other = spectra[array * rows : (array + 1) * rows]
            real, imag = other[:, :LANES], other[:, LANES:]
            part.append(
                jnp.concatenate([real * grad_real + imag * grad_imag, imag * grad_real - real * grad_imag], axis=1)
            )
        return split(jnp.concatenate(part))

    def turn_back(back):
        spread = []
        for array in range(2):
            value = back[array * rows : (array + 1) * rows]
            real, minus = value[:, :LANES], value[:, LANES:]
            spread.append(jnp.concatenate([real * cos + minus * sin, real * sin - minus * cos]))
        return split(jnp.concatenate(spread, axis=1))

    def narrow(value):
        both = dot(last_rows, value[0])
        return both[:height] + both[height:] + dot(last_rows[:height], value[1])

    turned = [turn_out(coarse[:, 3 * channel * LANES : 3 * (channel + 1) * LANES]) for channel in range(channels)]
    spectra = [wide(value) for value in turned]
    mixed = [mix(value) for value in spectra]
    back = [wide(value) for value in mixed]
    spread = [turn_back(value) for value in back]
    result = jnp.concatenate([narrow(value) for value in spread], axis=1)

    cells = height * channels
    total = sum(block[cells : 2 * cells] * block[2 * cells :] for block in blocks)
    owner = lax.broadcasted_iota(jnp.int32, total.shape, 0) % channels
    for channel in range(channels):
        grad_skip_ref[channel] = jnp.sum(jnp.where(owner == channel, total, 0.0))
        mine = pl.ds(channel, height, stride=channels)
        lanes = 2 * channel * LANES
        kept = skips[channel] * blocks[0][pl.ds(2 * cells + channel, height, stride=channels)]
        grad_signal_ref[mine, :] = result[:, lanes : lanes + LANES] + kept
        grad_filter_ref[mine, :] = result[:, lanes + LANES : lanes + 2 * LANES]


def dense(value):
    channels, cells = value.shape
    return value.reshape(channels, cells // LANES, LANES).transpose(1, 0, 2).reshape(-1, LANES)


def undense(value, channels):
    return value.reshape(-1, channels, LANES).transpose(1, 0, 2).reshape(channels, -1)


def gathered_body(signal, filter_taps, grad_out, skip):
    groups = lax.axis_size("seq")
    channels, cells = signal.shape
    length = cells * groups
    rows = length // LANES
    own = jnp.concatenate([dense(filter_taps), dense(signal), dense(grad_out)])
    cores = lax.axis_size("sub")
    steps = routes(groups, cores)
    arrived = []
    for targets in reversed(steps):
        hops = []
        for core, ahead in enumerate(targets):
            hops += [(device * cores + core, target * cores + core) for device, target in enumerate(ahead)]
        arrived.insert(0, lax.ppermute(own, ("seq", "sub"), hops))
    tables = [jnp.asarray(table) for table in gathered_tables(length, groups)]
    whole = pl.BlockSpec(memory_space=pltpu.VMEM)
    scalar = pl.BlockSpec(memory_space=pltpu.SMEM)
    params = pltpu.CompilerParams(vmem_limit_bytes=24 * 2**20)
    coarse = pl.pallas_call(
        functools.partial(own_kernel, channels),
        out_shape=jax.ShapeDtypeStruct((2 * rows, 3 * channels * LANES), jnp.float32),
        in_specs=[whole] * 5,
        out_specs=whole,
        compiler_params=params,
        cost_estimate=pl.CostEstimate(flops=2**27, bytes_accessed=2**21, transcendentals=0),
        name="own_part",
    )(own, *tables)
    coarse = pl.pallas_call(
        functools.partial(early_kernel, channels, steps[0]),
        out_shape=jax.ShapeDtypeStruct(coarse.shape, jnp.float32),
        in_specs=[whole] * 3,
        out_specs=whole,
        compiler_params=params,
        cost_estimate=pl.CostEstimate(flops=2**27, bytes_accessed=2**21, transcendentals=0),
        name="early_part",
    )(coarse, arrived[0], tables[0])
    shape = jax.ShapeDtypeStruct(dense(signal).shape, jnp.float32)
    grad_signal, grad_filter, grad_skip = pl.pallas_call(
        functools.partial(gathered_kernel, groups, channels, steps[1:]),
        out_shape=(shape, shape, jax.ShapeDtypeStruct((channels,), jnp.float32)),
        in_specs=[whole] + [whole] * (groups + 5),
        out_specs=(whole, whole, scalar),
        compiler_params=params,
        name="correlate",
    )(skip, coarse, own, *arrived, *tables)
    return (undense(grad_signal, channels), undense(grad_filter, channels), grad_skip)


def frequency_order(groups):
    slots = jnp.arange(2 * groups, dtype=jnp.int32)
    halves = slots // 2
    return jnp.where(slots % 2 == 0, halves, jnp.where(halves == 0, groups, 2 * groups - halves))


def phase_table(left_index, right_index, period):
    product = left_index[:, None] * right_index[None, :] % period
    return 2.0 * math.pi / period * product.astype(jnp.float32)


def transform_tables(cells):
    inner_len = 128
    outer_len = cells // inner_len
    outer_range = jnp.arange(outer_len, dtype=jnp.int32)
    inner_range = jnp.arange(inner_len, dtype=jnp.int32)
    outer_phase = phase_table(outer_range, outer_range, outer_len)
    twist_phase = phase_table(outer_range, inner_range, cells)
    inner_phase = phase_table(inner_range, inner_range, inner_len)
    return (
        jnp.cos(outer_phase),
        jnp.sin(outer_phase),
        jnp.cos(twist_phase),
        jnp.sin(twist_phase),
        jnp.cos(inner_phase),
        jnp.sin(inner_phase),
    )


def complex_apply(real_part, imag_part, cos_table, sin_table, pattern, turning):
    first = jnp.einsum(pattern, real_part, cos_table, precision=highest) - turning * jnp.einsum(
        pattern, imag_part, sin_table, precision=highest
    )
    second = jnp.einsum(pattern, imag_part, cos_table, precision=highest) + turning * jnp.einsum(
        pattern, real_part, sin_table, precision=highest
    )
    return (first, second)


def forward_transform(real_part, imag_part, tables):
    outer_cos, outer_sin, twist_cos, twist_sin, inner_cos, inner_sin = tables
    outer_len = outer_cos.shape[0]
    inner_len = inner_cos.shape[0]
    initial = real_part.shape
    folded = initial[:-1] + (outer_len, inner_len)
    real_part = real_part.reshape(folded)
    imag_part = imag_part.reshape(folded)
    real_part, imag_part = complex_apply(
        real_part, imag_part, outer_cos, outer_sin, "...ab,ac->...cb", -1.0
    )
    real_part, imag_part = (
        real_part * twist_cos + imag_part * twist_sin,
        imag_part * twist_cos - real_part * twist_sin,
    )
    real_part, imag_part = complex_apply(
        real_part, imag_part, inner_cos, inner_sin, "...cb,bd->...cd", -1.0
    )
    return (real_part.reshape(initial), imag_part.reshape(initial))


def inverse_transform(real_part, imag_part, tables):
    outer_cos, outer_sin, twist_cos, twist_sin, inner_cos, inner_sin = tables
    outer_len = outer_cos.shape[0]
    inner_len = inner_cos.shape[0]
    initial = real_part.shape
    folded = initial[:-1] + (outer_len, inner_len)
    real_part = real_part.reshape(folded)
    imag_part = imag_part.reshape(folded)
    real_part, imag_part = complex_apply(
        real_part, imag_part, inner_cos, inner_sin, "...cd,bd->...cb", 1.0
    )
    real_part, imag_part = (
        real_part * twist_cos - imag_part * twist_sin,
        imag_part * twist_cos + real_part * twist_sin,
    )
    real_part, imag_part = complex_apply(
        real_part, imag_part, outer_cos, outer_sin, "...cb,ac->...ab", 1.0
    )
    return (real_part.reshape(initial), imag_part.reshape(initial))


def split_body(signal, filter_taps, grad_out, skip):
    groups = lax.axis_size("seq")
    device = lax.axis_index("seq")
    cells = signal.shape[1]
    width = cells // groups
    doubled = 2 * groups
    period = doubled * cells
    freq_slots = frequency_order(groups)
    tables = transform_tables(cells)
    stacked = jnp.stack([signal, filter_taps, grad_out])[:, :, None, :]
    columns = lax.all_to_all(stacked, "seq", split_axis=3, concat_axis=2, tiled=True)
    group_rows = jnp.arange(groups, dtype=jnp.int32)
    group_phase = phase_table(group_rows, freq_slots, doubled)
    group_cos = jnp.cos(group_phase)
    group_sin = jnp.sin(group_phase)
    real_part = jnp.einsum("acpj,pm->acmj", columns, group_cos, precision=highest)
    imag_part = -jnp.einsum("acpj,pm->acmj", columns, group_sin, precision=highest)
    residues = device * width + jnp.arange(width, dtype=jnp.int32)
    twist_phase = phase_table(freq_slots, residues, period)
    twist_cos = jnp.cos(twist_phase)
    twist_sin = jnp.sin(twist_phase)
    twisted_real = real_part * twist_cos + imag_part * twist_sin
    twisted_imag = imag_part * twist_cos - real_part * twist_sin
    outgoing = jnp.stack([twisted_real, twisted_imag], 1)
    spectra = lax.all_to_all(outgoing, "seq", split_axis=3, concat_axis=4, tiled=True)
    freq_real, freq_imag = forward_transform(spectra[:, 0], spectra[:, 1], tables)
    grad_real = freq_real[-1]
    grad_imag = freq_imag[-1]
    signal_real, signal_imag = (freq_real[0], freq_imag[0])
    filter_real, filter_imag = (freq_real[1], freq_imag[1])
    input_real = filter_real * grad_real + filter_imag * grad_imag
    input_imag = filter_real * grad_imag - filter_imag * grad_real
    taps_real = signal_real * grad_real + signal_imag * grad_imag
    taps_imag = signal_real * grad_imag - signal_imag * grad_real
    back_real = jnp.stack([input_real, taps_real])
    back_imag = jnp.stack([input_imag, taps_imag])
    inverse_real, inverse_imag = inverse_transform(back_real, back_imag, tables)
    full_range = jnp.arange(cells, dtype=jnp.int32)
    local_slots = lax.dynamic_slice_in_dim(freq_slots, 2 * device, 2)
    back_phase = phase_table(local_slots, full_range, period)
    back_cos = jnp.cos(back_phase)
    back_sin = jnp.sin(back_phase)
    turned_real = inverse_real * back_cos - inverse_imag * back_sin
    turned_imag = inverse_imag * back_cos + inverse_real * back_sin
    returning = jnp.stack([turned_real, turned_imag], 1)
    residue_rows = lax.all_to_all(returning, "seq", split_axis=4, concat_axis=3, tiled=True)
    scale = 1.0 / period
    real_out = (
        jnp.einsum("ncmj,pm->ncpj", residue_rows[:, 0], group_cos, precision=highest)
        - jnp.einsum("ncmj,pm->ncpj", residue_rows[:, 1], group_sin, precision=highest)
    ) * scale
    gathered = lax.all_to_all(real_out, "seq", split_axis=2, concat_axis=3, tiled=True)
    grad_signal = gathered[0, :, 0, :] + skip[:, None] * grad_out
    grad_filter = gathered[1, :, 0, :]
    grad_skip = lax.psum(jnp.sum(grad_out * signal, axis=1), "seq")
    return (grad_signal, grad_filter, grad_skip)


def body(signal, filter_taps, grad_out, skip):
    groups = lax.axis_size("seq")
    channels, cells = signal.shape
    whole_fits = channels * cells * groups <= 2**15
    if whole_fits and groups <= 8 and cells % (16 * LANES) == 0:
        return gathered_body(signal, filter_taps, grad_out, skip)
    return split_body(signal, filter_taps, grad_out, skip)
def solution(mesh):
    return jax.shard_map(
        body,
        mesh=mesh,
        in_specs=(
            P(("parts", "chan", "sub"), "seq"),
            P(("parts", "chan", "sub"), "seq"),
            P(("parts", "chan", "sub"), "seq"),
            P(("parts", "chan", "sub")),
        ),
        out_specs=(
            P(("parts", "chan", "sub"), "seq"),
            P(("parts", "chan", "sub"), "seq"),
            P(("parts", "chan", "sub")),
        ),
        check_vma=False,
    )
```
